32 devices in a mesh: seq: 16 (over z, x, core), ch: 2 (over y).
Axes of the slice: x: 2, y: 2, z: 4, core: 2. Of those that a mesh axis runs over, the one named last changes fastest.
Arguments:
- query_feat: bfloat16 [4096, 4096], P('seq', 'ch'), may hold values from -6 to 6
- key_feat: bfloat16 [4096, 4096], P('seq', 'ch'), may hold values from -6 to 6
- value_feat: bfloat16 [4096, 4096], P('seq', 'ch'), may hold values from -6 to 6
- short_filter: float32 [3, 3, 4096], P(None, None, 'ch'), may hold values from -3.5 to 3.5
- long_filter: float32 [2048, 4096], P('ch', 'seq'), may hold values from -0.09375 to 0.09375
- direct_gain: float32 [4096], P('ch'), may hold values from 0.25 to 1.5
- out_weight: bfloat16 [4096, 4096], P('seq', 'ch'), may hold values from -0.09375 to 0.09375
Outputs:
- layer_out: bfloat16 [4096, 4096], P('seq', 'ch')
The draws below stay inside these ranges and needn't reach their ends.
All inputs are finite; a program needn't handle non-finite values.
Results may differ from the reference program's by a relative error of at most 0.0049.
Values may be sent and summed in bfloat16 or wider, within the bound.
No kernel may reach another device: no remote copies, remote signals or barrier semaphores. Data moves between devices by JAX's collectives and lax.ppermute only.
A program may use at most 64 MiB of HBM per device.

```python
import jax
import jax.numpy as jnp
from jax import lax

D = 4096
TAPS = 3
TOK_DEV = 256
SEQ_LEN = 4096
FG = 2048
N_SEQ = 16


def shard_levels(rng, extent, split, least, largest):
    level, own = 1.0, jax.random.fold_in(rng, 6)
    for axis_at, shards_of in split:
        steps = jnp.exp(jax.random.uniform(jax.random.fold_in(own, axis_at), (shards_of,), jnp.float32, least / len(split), largest / len(split)))
        level = level * jnp.repeat(steps, extent[axis_at] // shards_of).reshape([-1 if axis == axis_at else 1 for axis in range(len(extent))])
    return level


def noise(own_key, extent, spread, bound, pieces=(), kind=jnp.bfloat16):
    level = shard_levels(own_key, extent, pieces, -0.22, 0.18) if pieces else 1.0
    drawn = jax.random.normal(own_key, extent, jnp.float32) * spread * level
    return jnp.minimum(jnp.maximum(drawn, -bound), bound).astype(kind)


def setup_inputs(seed: int = 0) -> dict:
    streams_of = jax.random.split(jax.random.key(seed), 8)
    return {
        "query_feat": noise(streams_of[0], (SEQ_LEN, D), 1.0, 6.0, ((0, 16), (1, 2))),
        "key_feat": noise(streams_of[1], (SEQ_LEN, D), 1.0, 6.0, ((0, 16), (1, 2))),
        "value_feat": noise(streams_of[2], (SEQ_LEN, D), 1.0, 6.0, ((0, 16), (1, 2))),
        "short_filter": noise(streams_of[3], (3, TAPS, D), TAPS ** -0.5, 3.5, ((2, 2),), jnp.float32),
        "long_filter": noise(streams_of[4], (FG, SEQ_LEN), SEQ_LEN ** -0.5, 0.09375, ((0, 2), (1, 16)), jnp.float32),
        "direct_gain": jnp.clip(0.25 + 1.25 * jax.random.uniform(streams_of[5], (D,), jnp.float32) ** shard_levels(streams_of[5], (D,), ((0, 2),), -0.2, 0.2), 0.25, 1.5),
        "out_weight": noise(streams_of[6], (D, D), D ** -0.5, 0.09375, ((0, 16), (1, 2))),
    }


def featurize(inputs, taps):
    seq_len = inputs.shape[0]
    padded = jnp.pad(inputs.astype(jnp.float32), ((TAPS - 1, 0), (0, 0)))
    total = jnp.zeros(inputs.shape, jnp.float32)
    for tap in range(TAPS):
        total = total + taps[tap] * padded[TAPS - 1 - tap:TAPS - 1 - tap + seq_len]
    return total


def reference(query_feat, key_feat, value_feat, short_filter, long_filter, direct_gain, out_weight):
    seq_len = TOK_DEV * N_SEQ
    block_width = 256 if D % 256 == 0 else D
    block_count = D // block_width

    def split_rows(array_in):
        return array_in.reshape(seq_len, block_count, block_width).transpose(1, 0, 2)

    def one_block(block_items):
        queries, keys_in, values_in, tap_weights, filters, gain_block = block_items
        query_short = featurize(queries, tap_weights[0])
        key_short = featurize(keys_in, tap_weights[1])
        value_short = featurize(values_in, tap_weights[2])
        mixed = key_short * value_short
        full_filters = jnp.repeat(filters, 2, axis=0).T
        spectrum = jnp.fft.rfft(mixed, n=2 * seq_len, axis=0) * jnp.fft.rfft(full_filters, n=2 * seq_len, axis=0)
        long_out = jnp.fft.irfft(spectrum, n=2 * seq_len, axis=0)[:seq_len]
        summed = long_out + gain_block * mixed
        return (query_short * summed).astype(jnp.bfloat16)

    short_blocks = short_filter.reshape(3, TAPS, block_count, block_width).transpose(2, 0, 1, 3)
    gated = lax.map(one_block, (split_rows(query_feat), split_rows(key_feat), split_rows(value_feat),
                                short_blocks,
                                long_filter.reshape(block_count, block_width // 2, seq_len),
                                direct_gain.reshape(block_count, block_width)))
    gated = gated.transpose(1, 0, 2).reshape(seq_len, D)
    return jnp.dot(gated, out_weight, preferred_element_type=jnp.float32).astype(jnp.bfloat16)
```

```python
import functools

import jax
import jax.numpy as jnp
from jax import lax
from jax.experimental import pallas as pl
from jax.experimental.pallas import tpu as pltpu
from jax.sharding import PartitionSpec as P


TAPS = 3
LANES = 128
PACK = 16


def shifted(block, axis, distance):
    devices = range(lax.axis_size(axis))
    route = [(i - distance, i) for i in devices if i - distance in devices]
    return lax.ppermute(block, axis, route)


def featurized(inputs, edge, taps):
    rows = inputs.astype(jnp.float32)
    index = lax.broadcasted_iota(jnp.int32, rows.shape, 0)
    total = taps[0:1] * rows
    for tap in range(1, TAPS):
        moved = pltpu.roll(rows, tap, 0)
        for row in range(tap):
            first = TAPS - 1 - tap + row
            moved = jnp.where(index == row, edge[first : first + 1], moved)
        total = total + taps[tap : tap + 1] * moved
    return total


def mix_kernel(key_ref, value_ref, edge_ref, short_ref, mixed_ref, turned_ref):
    edge = edge_ref[...].astype(jnp.float32)
    mixed = featurized(key_ref[...], edge[1], short_ref[1]) * featurized(
        value_ref[...], edge[2], short_ref[2]
    )
    mixed_ref[...] = mixed
    turned_ref[...] = mixed.T.astype(jnp.bfloat16)


def gate_kernel(query_ref, edge_ref, short_ref, gain_ref, mixed_ref, conv_ref, gated_ref):
    edge = edge_ref[...].astype(jnp.float32)
    query_short = featurized(query_ref[...], edge[0], short_ref[0])
    summed = conv_ref[...].astype(jnp.float32).T + gain_ref[...] * mixed_ref[...]
    gated_ref[...] = (query_short * summed).astype(jnp.bfloat16)


def conv_kernel(n, tok, width, x_ref, f_ref, y_ref, xi, xs, ys):
    halves = tok // LANES
    groups = LANES // PACK
    for e in range(halves):
        for i in range(n):
            xi[e, i * width : (i + 1) * width, :] = x_ref[
                i, :, e * LANES : (e + 1) * LANES
            ].astype(jnp.float32)
        for c in range(width):
            xs[e, c, 0:n, :] = jnp.zeros((n, LANES), jnp.float32)
            xs[e, c, n : 2 * n, :] = xi[e, pl.ds(c, n, stride=width), :]
    lane = lax.broadcasted_iota(jnp.int32, (PACK, LANES), 1)
    sub = lax.broadcasted_iota(jnp.int32, (PACK, LANES), 0)

    def one(p, carry):
        def skewed(m):
            if m == 0:
                return jnp.zeros((PACK, LANES), jnp.float32)
            row = f_ref[p, m - 1 : m, :]
            return pltpu.roll(
                jnp.broadcast_to(row, (PACK, LANES)), 0, 1, stride=1, stride_axis=0
            )

        def turns(m, part):
            now = skewed(m)
            base = jnp.where(lane >= sub, now, part).astype(jnp.bfloat16)
            return now, [base] + [
                pltpu.roll(base, LANES - PACK * k, 1) for k in range(1, groups)
            ]

        def stack(before, after):
            tiles = [after[0]]
            for k in range(groups - 1, 0, -1):
                tiles.append(jnp.where(lane < LANES - PACK * k, before[k], after[k]))
            return jnp.concatenate(tiles, axis=0)

        part, before = turns(0, skewed(0))
        old = jnp.zeros((LANES, LANES), jnp.bfloat16)
        acc = None
        for d in range(n):
            cols = [old]
            for e in range(halves):
                part, after = turns(d * halves + e + 1, part)
                cols.append(stack(before, after))
                before = after
            old = cols[-1]
            rhs = jnp.concatenate(
                [jnp.concatenate(cols[1:], axis=1), jnp.concatenate(cols[:-1], axis=1)], axis=0
            )
            lhs = jnp.concatenate(
                [
                    jnp.concatenate(
                        [
                            xs[e, 2 * p + c, n - d : 2 * n - d, :].astype(jnp.bfloat16)
                            for e in range(halves)
                        ],
                        axis=1,
                    )
                    for c in range(2)
                ],
                axis=0,
            )
            out = jnp.dot(lhs, rhs, preferred_element_type=jnp.float32)
            acc = out if acc is None else acc + out
        for e in range(halves):
            for c in range(2):
                ys[e, pl.ds(2 * p + c, n, stride=width), :] = acc[
                    c * n : (c + 1) * n, e * LANES : (e + 1) * LANES
                ]
        return carry

    lax.fori_loop(0, width // 2, one, 0, unroll=4 if n <= 16 else 1)
    for e in range(halves):
        for i in range(n):
            y_ref[i, :, e * LANES : (e + 1) * LANES] = ys[
                e, i * width : (i + 1) * width, :
            ].astype(jnp.bfloat16)


def convolve(x, f):
    n, chans, tok = x.shape
    width = min(16, chans)
    halves = tok // LANES
    assert halves == 2
    return pl.pallas_call(
        functools.partial(conv_kernel, n, tok, width),
        grid=(chans // width,),
        in_specs=[
            pl.BlockSpec((n, width, tok), lambda g: (0, g, 0)),
            pl.BlockSpec((width // 2, n * halves, LANES), lambda g: (g, 0, 0)),
        ],
        out_specs=pl.BlockSpec((n, width, tok), lambda g: (0, g, 0)),
        out_shape=jax.ShapeDtypeStruct(x.shape, jnp.bfloat16),
        scratch_shapes=[
            pltpu.VMEM((halves, n * width, LANES), jnp.float32),
            pltpu.VMEM((halves, width, 2 * n, LANES), jnp.float32),
            pltpu.VMEM((halves, n * width, LANES), jnp.float32),
        ],
        name="convolve",
    )(x, f)


def mix(key_feat, value_feat, edges, short_filter):
    tokens, channels = key_feat.shape
    wide = min(512, channels)
    rows = pl.BlockSpec((tokens, wide), lambda g: (0, g))
    return pl.pallas_call(
        mix_kernel,
        grid=(channels // wide,),
        in_specs=[
            rows,
            rows,
            pl.BlockSpec((3, TAPS - 1, wide), lambda g: (0, 0, g)),
            pl.BlockSpec((3, TAPS, wide), lambda g: (0, 0, g)),
        ],
        out_specs=[rows, pl.BlockSpec((wide, tokens), lambda g: (g, 0))],
        out_shape=[
            jax.ShapeDtypeStruct((tokens, channels), jnp.float32),
            jax.ShapeDtypeStruct((channels, tokens), jnp.bfloat16),
        ],
        name="mix",
    )(key_feat, value_feat, edges, short_filter)


def gate(query_feat, edges, short_filter, gain, mixed, conv):
    tokens, channels = query_feat.shape
    wide = min(512, channels)
    rows = pl.BlockSpec((tokens, wide), lambda g: (0, g))
    return pl.pallas_call(
        gate_kernel,
        grid=(channels // wide,),
        in_specs=[
            rows,
            pl.BlockSpec((3, TAPS - 1, wide), lambda g: (0, 0, g)),
            pl.BlockSpec((3, TAPS, wide), lambda g: (0, 0, g)),
            pl.BlockSpec((1, wide), lambda g: (0, g)),
            rows,
            pl.BlockSpec((wide, tokens), lambda g: (g, 0)),
        ],
        out_specs=rows,
        out_shape=jax.ShapeDtypeStruct((tokens, channels), jnp.bfloat16),
        name="gate",
    )(query_feat, edges, short_filter, gain, mixed, conv)


def local(query_feat, key_feat, value_feat, short_filter, long_filter, direct_gain, out_weight):
  if True:
    tokens, channels = query_feat.shape
    devices = lax.axis_size("seq")
    sides = lax.axis_size("ch")
    with jax.named_scope("wgather"):
        weights = lax.all_gather(out_weight, "seq", axis=0, tiled=True)
    with jax.named_scope("edge"):
        last = slice(tokens - (TAPS - 1), None)
        edges = shifted(jnp.stack([query_feat[last], key_feat[last], value_feat[last]]), "seq", 1)
    with jax.named_scope("filters"):
        pairs = long_filter.shape[0] // devices
        sent = long_filter.astype(jnp.bfloat16).reshape(devices, pairs, tokens)
        taps = lax.all_to_all(sent, "seq", split_axis=0, concat_axis=0, tiled=True)
        taps = taps.astype(jnp.float32).transpose(1, 0, 2)
        taps = taps.reshape(pairs, devices * tokens // LANES, LANES)
    with jax.named_scope("mix"):
        mixed, turned = mix(key_feat, value_feat, edges, short_filter)
    with jax.named_scope("spread"):
        spread = lax.all_to_all(
            turned.reshape(devices, 2 * pairs, tokens), "seq", split_axis=0, concat_axis=0, tiled=True
        )
    with jax.named_scope("conv"):
        conv = convolve(spread, taps)
    with jax.named_scope("back"):
        long_out = lax.all_to_all(conv, "seq", split_axis=0, concat_axis=0, tiled=True)
    with jax.named_scope("gate"):
        gated = gate(query_feat, edges, short_filter, direct_gain[None], mixed, long_out.reshape(channels, tokens))
    with jax.named_scope("swap"):
        place = lax.axis_index("ch")
        pieces = [gated]
        for step in range(1, sides):
            route = [((i + step) % sides, i) for i in range(sides)]
            pieces.append(lax.ppermute(gated, "ch", route))
    with jax.named_scope("project"):
        if sides == 2:
            first = jnp.where(place == 0, pieces[0], pieces[1])
            second = jnp.where(place == 0, pieces[1], pieces[0])
            features = jnp.concatenate([first, second], axis=1)
        else:
            stacked = jnp.concatenate(pieces + pieces, axis=1)
            features = lax.dynamic_slice_in_dim(stacked, (sides - place) % sides * channels, sides * channels, 1)
        result = jnp.dot(features, weights, preferred_element_type=jnp.float32)
        return result.astype(jnp.bfloat16)


def solution(mesh):
    in_specs = (
        P("seq", "ch"),
        P("seq", "ch"),
        P("seq", "ch"),
        P(None, None, "ch"),
        P("ch", "seq"),
        P("ch"),
        P("seq", "ch"),
    )
    step = jax.shard_map(local, mesh=mesh, in_specs=in_specs, out_specs=P("seq", "ch"), check_vma=False)
    return step
```

```python
import functools

import jax
import jax.numpy as jnp
from jax import lax
from jax.experimental import pallas as pl
from jax.experimental.pallas import tpu as pltpu
from jax.sharding import PartitionSpec as P


TAPS = 3
PARTS = 2
LANES = 128
PACK = 16


def shifted(block, axis, distance):
    devices = range(lax.axis_size(axis))
    route = [(i - distance, i) for i in devices if i - distance in devices]
    return lax.ppermute(block, axis, route)


def featurized(inputs, edge, taps):
    rows = inputs.astype(jnp.float32)
    index = lax.broadcasted_iota(jnp.int32, rows.shape, 0)
    total = taps[0:1] * rows
    for tap in range(1, TAPS):
        moved = pltpu.roll(rows, tap, 0)
        for row in range(tap):
            first = TAPS - 1 - tap + row
            moved = jnp.where(index == row, edge[first : first + 1], moved)
        total = total + taps[tap : tap + 1] * moved
    return total


def mix_kernel(key_ref, value_ref, edge_ref, short_ref, mixed_ref, turned_ref):
    edge = edge_ref[...].astype(jnp.float32)
    mixed = featurized(key_ref[...], edge[1], short_ref[1]) * featurized(
        value_ref[...], edge[2], short_ref[2]
    )
    mixed_ref[...] = mixed
    turned_ref[...] = mixed.T.astype(jnp.bfloat16)


def gate_kernel(query_ref, edge_ref, short_ref, gain_ref, mixed_ref, conv_ref, gated_ref):
    edge = edge_ref[...].astype(jnp.float32)
    query_short = featurized(query_ref[...], edge[0], short_ref[0])
    summed = conv_ref[...].astype(jnp.float32).T + gain_ref[...] * mixed_ref[...]
    gated_ref[0] = (query_short * summed).astype(jnp.bfloat16)


def conv_kernel(n, tok, width, x_ref, f_ref, y_ref, xi, xs, ys):
    halves = tok // LANES
    groups = LANES // PACK
    for e in range(halves):
        for i in range(n):
            xi[e, i * width : (i + 1) * width, :] = x_ref[
                i, :, e * LANES : (e + 1) * LANES
            ].astype(jnp.float32)
        for c in range(width):
            xs[e, c, 0:n, :] = jnp.zeros((n, LANES), jnp.float32)
            xs[e, c, n : 2 * n, :] = xi[e, pl.ds(c, n, stride=width), :]
    lane = lax.broadcasted_iota(jnp.int32, (PACK, LANES), 1)
    sub = lax.broadcasted_iota(jnp.int32, (PACK, LANES), 0)

    def one(p, carry):
        def skewed(m):
            if m == 0:
                return jnp.zeros((PACK, LANES), jnp.float32)
            row = f_ref[p, m - 1 : m, :]
            return pltpu.roll(
                jnp.broadcast_to(row, (PACK, LANES)), 0, 1, stride=1, stride_axis=0
            )

        def turns(m, part):
            now = skewed(m)
            base = jnp.where(lane >= sub, now, part).astype(jnp.bfloat16)
            return now, [base] + [
                pltpu.roll(base, LANES - PACK * k, 1) for k in range(1, groups)
            ]

        def stack(before, after):
            tiles = [after[0]]
            for k in range(groups - 1, 0, -1):
                tiles.append(jnp.where(lane < LANES - PACK * k, before[k], after[k]))
            return jnp.concatenate(tiles, axis=0)

        part, before = turns(0, skewed(0))
        old = jnp.zeros((LANES, LANES), jnp.bfloat16)
        acc = None
        for d in range(n):
            cols = [old]
            for e in range(halves):
                part, after = turns(d * halves + e + 1, part)
                cols.append(stack(before, after))
                before = after
            old = cols[-1]
            rhs = jnp.concatenate(
                [jnp.concatenate(cols[1:], axis=1), jnp.concatenate(cols[:-1], axis=1)], axis=0
            )
            lhs = jnp.concatenate(
                [
                    jnp.concatenate(
                        [
                            xs[e, 2 * p + c, n - d : 2 * n - d, :].astype(jnp.bfloat16)
                            for e in range(halves)
                        ],
                        axis=1,
                    )
                    for c in range(2)
                ],
                axis=0,
            )
            out = jnp.dot(lhs, rhs, preferred_element_type=jnp.float32)
            acc = out if acc is None else acc + out
        for e in range(halves):
            for c in range(2):
                ys[e, pl.ds(2 * p + c, n, stride=width), :] = acc[
                    c * n : (c + 1) * n, e * LANES : (e + 1) * LANES
                ]
        return carry

    lax.fori_loop(0, width // 2, one, 0, unroll=4 if n <= 16 else 1)
    for e in range(halves):
        for i in range(n):
            y_ref[i, :, e * LANES : (e + 1) * LANES] = ys[
                e, i * width : (i + 1) * width, :
            ].astype(jnp.bfloat16)


def convolve(x, f, part):
    n, chans, tok = x.shape
    width = min(16, chans)
    halves = tok // LANES
    assert halves == 2
    return pl.pallas_call(
        functools.partial(conv_kernel, n, tok, width),
        grid=(chans // width,),
        in_specs=[
            pl.BlockSpec((n, width, tok), lambda g: (0, g, 0)),
            pl.BlockSpec(
                (width // 2, n * halves, LANES), lambda g: (g + part * (chans // width), 0, 0)
            ),
        ],
        out_specs=pl.BlockSpec((n, width, tok), lambda g: (0, g, 0)),
        out_shape=jax.ShapeDtypeStruct(x.shape, jnp.bfloat16),
        scratch_shapes=[
            pltpu.VMEM((halves, n * width, LANES), jnp.float32),
            pltpu.VMEM((halves, width, 2 * n, LANES), jnp.float32),
            pltpu.VMEM((halves, n * width, LANES), jnp.float32),
        ],
        name="convolve",
    )(x, f)


def mix(key_feat, value_feat, edges, short_filter, part, parts):
    tokens, channels = key_feat.shape
    channels //= parts
    wide = min(512, channels)
    first = part * (channels // wide)
    rows = pl.BlockSpec((tokens, wide), lambda g: (0, g + first))
    return pl.pallas_call(
        mix_kernel,
        grid=(channels // wide,),
        in_specs=[
            rows,
            rows,
            pl.BlockSpec((3, TAPS - 1, wide), lambda g: (0, 0, g + first)),
            pl.BlockSpec((3, TAPS, wide), lambda g: (0, 0, g + first)),
        ],
        out_specs=[
            pl.BlockSpec((tokens, wide), lambda g: (0, g)),
            pl.BlockSpec((wide, tokens), lambda g: (g, 0)),
        ],
        out_shape=[
            jax.ShapeDtypeStruct((tokens, channels), jnp.float32),
            jax.ShapeDtypeStruct((channels, tokens), jnp.bfloat16),
        ],
        name="mix",
    )(key_feat, value_feat, edges, short_filter)


def gate(query_feat, edges, short_filter, gain, mixed, conv, part, wide):
    tokens, channels = mixed.shape
    first = part * (channels // wide)
    return pl.pallas_call(
        gate_kernel,
        grid=(channels // wide,),
        in_specs=[
            pl.BlockSpec((tokens, wide), lambda g: (0, g + first)),
            pl.BlockSpec((3, TAPS - 1, wide), lambda g: (0, 0, g + first)),
            pl.BlockSpec((3, TAPS, wide), lambda g: (0, 0, g + first)),
            pl.BlockSpec((1, wide), lambda g: (0, g + first)),
            pl.BlockSpec((tokens, wide), lambda g: (0, g)),
            pl.BlockSpec((wide, tokens), lambda g: (g, 0)),
        ],
        out_specs=pl.BlockSpec((1, tokens, wide), lambda g: (g, 0, 0)),
        out_shape=jax.ShapeDtypeStruct((channels // wide, tokens, wide), jnp.bfloat16),
        name="gate",
    )(query_feat, edges, short_filter, gain, mixed, conv)


def project_kernel(count, parts, spots, *refs):
    per = 4 * parts
    gated, pieces = refs[:per], refs[per : per + count]
    own_ref, far_ref, rows = refs[per + count :]
    tokens, wide = gated[0].shape[1:]
    blocks = gated[0].shape[0]

    @pl.when(pl.program_id(0) == 0)
    def _():
        for piece in range(count):
            spot = spots[piece]
            for part in range(parts):
                @pl.when(lax.rem(spot, blocks * parts) // blocks == part)
                def _():
                    index = lax.rem(spot, blocks)
                    near = spot < blocks * parts
                    for token in range(2):
                        own, other = gated[(2 * token) * parts + part], gated[(2 * token + 1) * parts + part]
                        rows[token * tokens : (token + 1) * tokens, piece * wide : (piece + 1) * wide] = jnp.where(
                            near, own[index], other[index]
                        )

    total = None
    for piece in range(count):
        out = jnp.dot(
            rows[:, piece * wide : (piece + 1) * wide], pieces[piece][...], preferred_element_type=jnp.float32
        )
        total = out if total is None else total + out
    own_ref[...] = total[:tokens].astype(jnp.bfloat16)
    far_ref[...] = total[tokens:].astype(jnp.bfloat16)


def project(spots, gated, pieces, parts):
    blocks, tokens, wide = gated[0].shape
    count = len(pieces)
    columns = pieces[0].shape[1]
    step = min(256, columns)
    whole = pl.BlockSpec((blocks, tokens, wide), lambda j, spots: (0, 0, 0))
    out = pl.BlockSpec((tokens, step), lambda j, spots: (0, j))
    return pl.pallas_call(
        functools.partial(project_kernel, count, parts),
        grid_spec=pltpu.PrefetchScalarGridSpec(
            num_scalar_prefetch=1,
            grid=(columns // step,),
            in_specs=[whole] * len(gated)
            + [pl.BlockSpec((wide, step), lambda j, spots: (0, j))] * count,
            out_specs=[out, out],
            scratch_shapes=[pltpu.VMEM((2 * tokens, count * wide), jnp.bfloat16)],
        ),
        out_shape=[jax.ShapeDtypeStruct((tokens, columns), jnp.bfloat16)] * 2,
        name="project",
    )(spots, *gated, *pieces)


def local(query_feat, key_feat, value_feat, short_filter, long_filter, direct_gain, out_weight):
    tokens, channels = query_feat.shape
    devices = lax.axis_size("seq")
    sides = lax.axis_size("ch")
    here = lax.axis_index("seq")
    place = lax.axis_index("ch")
    depth, columns = out_weight.shape
    pairs = long_filter.shape[0] // devices
    small = sides == 2 and depth % 256 == 0
    parts = PARTS if small else 1

    core_swap = [(i ^ 1, i) for i in range(devices)]
    near_swap = [(i ^ 2, i) for i in range(devices)]
    up = [(i, i + 4) for i in range(devices - 4)]
    down = [(i + 4, i) for i in range(devices - 4)]
    side_swap = [(i ^ 1, i) for i in range(sides)]

    with jax.named_scope("edge"):
        last = slice(tokens - (TAPS - 1), None)
        edges = shifted(jnp.stack([query_feat[last], key_feat[last], value_feat[last]]), "seq", 1)

    if small:
        with jax.named_scope("weights"):
            line = devices // 4
            level = here // 4
            half = columns // 2
            core = here % 2
            mine = lax.dynamic_slice_in_dim(out_weight, core * half, half, 1)
            theirs = lax.dynamic_slice_in_dim(out_weight, (1 - core) * half, half, 1)
            theirs = lax.ppermute(theirs, "seq", core_swap)
            pieces, spots = [], []
            for flip, start in ((0, mine), (1, theirs)):
                rising, falling = [start], [start]
                for _ in range(line - 1):
                    rising.append(lax.ppermute(rising[-1], "seq", up))
                    falling.append(lax.ppermute(falling[-1], "seq", down))
                for step in range(line):
                    block = start if step == 0 else jnp.where(level >= step, rising[step], falling[line - step])
                    owner = (level - step) % line * 4 + here % 4
                    for turn, piece in ((0, block), (2, lax.ppermute(block, "seq", near_swap))):
                        pieces.append(piece)
                        spots.append(owner ^ flip ^ turn)
            blocks = channels // depth
            spots = jnp.stack([(spot // blocks != place) * blocks + spot % blocks for spot in spots]).astype(jnp.int32)
    else:
        with jax.named_scope("weights"):
            weights = lax.all_gather(out_weight, "seq", axis=0, tiled=True)

    with jax.named_scope("filters"):
        sent = long_filter.astype(jnp.bfloat16).reshape(parts, devices, pairs // parts, tokens)
        sent = sent.transpose(1, 0, 2, 3).reshape(devices, pairs, tokens)
        taps = lax.all_to_all(sent, "seq", split_axis=0, concat_axis=0, tiled=True)
        taps = taps.astype(jnp.float32).transpose(1, 0, 2)
        taps = taps.reshape(pairs, devices * tokens // LANES, LANES)

    gain = direct_gain[None]
    wide = min(256, depth) if small else min(256, channels)
    mixes, spreads, convs, gateds = [], [], [], []
    for part in range(parts):
        mixes.append(mix(key_feat, value_feat, edges, short_filter, part, parts))
    for part in range(parts):
        turned = mixes[part][1].reshape(devices, 2 * pairs // parts, tokens)
        spreads.append(lax.all_to_all(turned, "seq", split_axis=0, concat_axis=0, tiled=True))
    for part in range(parts):
        convs.append(lax.all_to_all(convolve(spreads[part], taps, part), "seq", split_axis=0, concat_axis=0, tiled=True))
    for part in range(parts):
        gateds.append(
            gate(
                query_feat, edges, short_filter, gain, mixes[part][0], convs[part].reshape(channels // parts, tokens), part, wide
            )
        )

    if small:
        own = gateds
        other = [lax.ppermute(g, "ch", side_swap) for g in own]
        far_own = [lax.ppermute(g, "seq", core_swap) for g in own]
        far_other = [lax.ppermute(g, "seq", core_swap) for g in other]
        kept, given = project(spots, own + other + far_own + far_other, pieces, parts)
        taken = lax.ppermute(given, "seq", core_swap)
        low = jnp.where(core == 0, kept, taken)
        high = jnp.where(core == 0, taken, kept)
        return jnp.concatenate([low, high], axis=1)

    gated = gateds[0].transpose(1, 0, 2).reshape(tokens, channels)
    features = lax.all_gather(gated, "ch", axis=1, tiled=True)
    return jnp.dot(features, weights, preferred_element_type=jnp.float32).astype(jnp.bfloat16)


def solution(mesh):
    in_specs = (
        P("seq", "ch"),
        P("seq", "ch"),
        P("seq", "ch"),
        P(None, None, "ch"),
        P("ch", "seq"),
        P("ch"),
        P("seq", "ch"),
    )
    return jax.shard_map(
        local, mesh=mesh, in_specs=in_specs, out_specs=P("seq", "ch"), check_vma=False
    )
```

```python
import functools

import jax
import jax.numpy as jnp
from jax import lax
from jax.experimental import pallas as pl
from jax.experimental.pallas import tpu as pltpu
from jax.sharding import PartitionSpec as P


TAPS = 3
PARTS = 2
LANES = 128
PACK = 16


def shifted(block, axis, distance):
    devices = range(lax.axis_size(axis))
    route = [(i - distance, i) for i in devices if i - distance in devices]
    return lax.ppermute(block, axis, route)


def featurized(inputs, edge, taps):
    rows = inputs.astype(jnp.float32)
    index = lax.broadcasted_iota(jnp.int32, rows.shape, 0)
    total = taps[0:1] * rows
    for tap in range(1, TAPS):
        moved = pltpu.roll(rows, tap, 0)
        for row in range(tap):
            first = TAPS - 1 - tap + row
            moved = jnp.where(index == row, edge[first : first + 1], moved)
        total = total + taps[tap : tap + 1] * moved
    return total


def mix_kernel(key_ref, value_ref, edge_ref, short_ref, turned_ref):
    edge = edge_ref[...].astype(jnp.float32)
    mixed = featurized(key_ref[...], edge[1], short_ref[1]) * featurized(
        value_ref[...], edge[2], short_ref[2]
    )
    turned_ref[...] = mixed.T.astype(jnp.bfloat16).reshape(turned_ref.shape)


def gate_kernel(query_ref, edge_ref, short_ref, conv_ref, gated_ref):
    edge = edge_ref[...].astype(jnp.float32)
    query_short = featurized(query_ref[...], edge, short_ref[0])
    summed = conv_ref[...].astype(jnp.float32).reshape(query_short.shape[1], query_short.shape[0]).T
    gated_ref[0] = (query_short * summed).astype(jnp.bfloat16)


def conv_kernel(n, tok, width, place, x_ref, f_ref, gain_ref, y_ref, xi, xs, ys):
    halves = tok // LANES
    groups = LANES // PACK
    for e in range(halves):
        for i in range(n):
            xi[e, i * width : (i + 1) * width, :] = x_ref[
                i, :, e * LANES : (e + 1) * LANES
            ].astype(jnp.float32)
        for c in range(width):
            xs[e, c, 0:n, :] = jnp.zeros((n, LANES), jnp.float32)
            xs[e, c, n : 2 * n, :] = xi[e, pl.ds(c, n, stride=width), :]
    lane = lax.broadcasted_iota(jnp.int32, (PACK, LANES), 1)
    sub = lax.broadcasted_iota(jnp.int32, (PACK, LANES), 0)

    def one(p, carry):
        def skewed(m):
            if m == 0:
                return jnp.zeros((PACK, LANES), jnp.float32)
            row = f_ref[p, m - 1 : m, :]
            return pltpu.roll(
                jnp.broadcast_to(row, (PACK, LANES)), 0, 1, stride=1, stride_axis=0
            )

        def turns(m, part):
            now = skewed(m)
            base = jnp.where(lane >= sub, now, part).astype(jnp.bfloat16)
            return now, [base] + [
                pltpu.roll(base, LANES - PACK * k, 1) for k in range(1, groups)
            ]

        def stack(before, after):
            tiles = [after[0]]
            for k in range(groups - 1, 0, -1):
                tiles.append(jnp.where(lane < LANES - PACK * k, before[k], after[k]))
            return jnp.concatenate(tiles, axis=0)

        part, before = turns(0, skewed(0))
        old = jnp.zeros((LANES, LANES), jnp.bfloat16)
        acc = None
        for d in range(n):
            cols = [old]
            for e in range(halves):
                part, after = turns(d * halves + e + 1, part)
                cols.append(stack(before, after))
                before = after
            old = cols[-1]
            rhs = jnp.concatenate(
                [jnp.concatenate(cols[1:], axis=1), jnp.concatenate(cols[:-1], axis=1)], axis=0
            )
            lhs = jnp.concatenate(
                [
                    jnp.concatenate(
                        [
                            xs[e, 2 * p + c, n - d : 2 * n - d, :].astype(jnp.bfloat16)
                            for e in range(halves)
                        ],
                        axis=1,
                    )
                    for c in range(2)
                ],
                axis=0,
            )
            out = jnp.dot(lhs, rhs, preferred_element_type=jnp.float32)
            acc = out if acc is None else acc + out
        for e in range(halves):
            for c in range(2):
                ys[e, pl.ds(2 * p + c, n, stride=width), :] = acc[
                    c * n : (c + 1) * n, e * LANES : (e + 1) * LANES
                ]
        return carry

    lax.fori_loop(0, width // 2, one, 0, unroll=4 if n <= 16 else 1)
    for e in range(halves):
        for i in range(n):
            rows = slice(i * width, (i + 1) * width)
            total = ys[e, rows, :] + gain_ref[...] * xi[e, rows, :]
            y_ref[place(i), :, e * LANES : (e + 1) * LANES] = total.astype(jnp.bfloat16)


def convolve(x, f, gain, part, place):
    n, chans, tok = x.shape
    width = min(16, chans)
    halves = tok // LANES
    assert halves == 2
    return pl.pallas_call(
        functools.partial(conv_kernel, n, tok, width, place),
        grid=(chans // width,),
        in_specs=[
            pl.BlockSpec((n, width, tok), lambda g: (0, g, 0)),
            pl.BlockSpec(
                (width // 2, n * halves, LANES), lambda g: (g + part * (chans // width), 0, 0)
            ),
            pl.BlockSpec((width, LANES), lambda g: (g + part * (chans // width), 0)),
        ],
        out_specs=pl.BlockSpec((n, width, tok), lambda g: (0, g, 0)),
        out_shape=jax.ShapeDtypeStruct(x.shape, jnp.bfloat16),
        scratch_shapes=[
            pltpu.VMEM((halves, n * width, LANES), jnp.float32),
            pltpu.VMEM((halves, width, 2 * n, LANES), jnp.float32),
            pltpu.VMEM((halves, n * width, LANES), jnp.float32),
        ],
        name="convolve",
    )(x, f, gain)


def mix(key_feat, value_feat, edges, short_filter, part, parts, outer, inner):
    tokens, channels = key_feat.shape
    wide = channels // (2 * parts)
    return pl.pallas_call(
        mix_kernel,
        grid=(2,),
        in_specs=[
            pl.BlockSpec((tokens, wide), lambda g: (0, g * parts + part)),
            pl.BlockSpec((tokens, wide), lambda g: (0, g * parts + part)),
            pl.BlockSpec((3, TAPS - 1, wide), lambda g: (0, 0, g * parts + part)),
            pl.BlockSpec((3, TAPS, wide), lambda g: (0, 0, g * parts + part)),
        ],
        out_specs=pl.BlockSpec(
            (outer, 1, inner, wide // (outer * inner), tokens), lambda g: (0, g, 0, 0, 0)
        ),
        out_shape=jax.ShapeDtypeStruct(
            (outer, 2, inner, wide // (outer * inner), tokens), jnp.bfloat16
        ),
        name="mix",
    )(key_feat, value_feat, edges, short_filter)


def gate(spot, query, edge, short_filter, conv, first, wide):
    sources, _, each, tokens = conv.shape
    blocks = sources * each // wide
    per = wide // each
    return pl.pallas_call(
        lambda spot_ref, *refs: gate_kernel(*refs),
        grid_spec=pltpu.PrefetchScalarGridSpec(
            num_scalar_prefetch=1,
            grid=(blocks,),
            in_specs=[
                pl.BlockSpec((tokens, wide), lambda g, spot: (0, spot[0] + g + first * blocks)),
                pl.BlockSpec((TAPS - 1, wide), lambda g, spot: (0, spot[0] + g + first * blocks)),
                pl.BlockSpec((3, TAPS, wide), lambda g, spot: (0, 0, spot[1] + g + first * blocks)),
                pl.BlockSpec((per, 1, each, tokens), lambda g, spot: (g, spot[2], 0, 0)),
            ],
            out_specs=pl.BlockSpec((1, tokens, wide), lambda g, spot: (g, 0, 0)),
        ),
        out_shape=jax.ShapeDtypeStruct((blocks, tokens, wide), jnp.bfloat16),
        name="gate",
    )(spot, query, edge, short_filter, conv)


def plain(query_feat, key_feat, value_feat, short_filter, long_filter, direct_gain, out_weight):
    tokens, channels = query_feat.shape
    devices = lax.axis_size("seq")
    pairs = long_filter.shape[0] // devices
    here = lax.axis_index("seq")
    weights = lax.all_gather(out_weight, "seq", axis=0, tiled=True)
    last = slice(tokens - (TAPS - 1), None)
    edges = shifted(jnp.stack([query_feat[last], key_feat[last], value_feat[last]]), "seq", 1)
    sent = long_filter.astype(jnp.bfloat16).reshape(devices, pairs, tokens)
    taps = lax.all_to_all(sent, "seq", split_axis=0, concat_axis=0, tiled=True)
    taps = taps.astype(jnp.float32).transpose(1, 0, 2)
    taps = taps.reshape(pairs, devices * tokens // LANES, LANES)
    gain = lax.dynamic_index_in_dim(direct_gain.reshape(devices, 2 * pairs, 1), here, 0, False)
    gain = jnp.broadcast_to(gain, (2 * pairs, LANES))
    turned = mix(key_feat, value_feat, edges, short_filter, 0, 1, 1, devices // 2)
    turned = turned.reshape(devices, 2 * pairs, tokens)
    spread = lax.all_to_all(turned, "seq", split_axis=0, concat_axis=0, tiled=True)
    conv = convolve(spread, taps, gain, 0, lambda i: i)
    conv = lax.all_to_all(conv, "seq", split_axis=0, concat_axis=0, tiled=True)
    wide = min(256, channels)
    spot = jnp.zeros((3,), jnp.int32)
    gated = gate(spot, query_feat, edges[0], short_filter, conv[:, None], 0, wide)
    gated = gated.transpose(1, 0, 2).reshape(tokens, channels)
    features = lax.all_gather(gated, "ch", axis=1, tiled=True)
    return jnp.dot(features, weights, preferred_element_type=jnp.float32).astype(jnp.bfloat16)


def project_kernel(count, parts, spots, *refs):
    gated, pieces = refs[: 2 * parts], refs[2 * parts : 2 * parts + count]
    out_ref, rows = refs[2 * parts + count :]
    blocks, _, wide = gated[0].shape

    @pl.when(pl.program_id(0) == 0)
    def _():
        for piece in range(count):
            spot = spots[piece]
            for source in range(2 * parts):

                @pl.when(spot // blocks == source)
                def _():
                    rows[:, piece * wide : (piece + 1) * wide] = gated[source][lax.rem(spot, blocks)]

    total = None
    for piece in range(count):
        out = jnp.dot(
            rows[:, piece * wide : (piece + 1) * wide],
            pieces[piece][...],
            preferred_element_type=jnp.float32,
        )
        total = out if total is None else total + out
    out_ref[...] = total.astype(out_ref.dtype)


def project(spots, gated, pieces, parts, kind):
    blocks, tokens, wide = gated[0].shape
    count = len(pieces)
    columns = pieces[0].shape[1]
    step = min(512, columns)
    whole = pl.BlockSpec((blocks, tokens, wide), lambda j, spots: (0, 0, 0))
    return pl.pallas_call(
        functools.partial(project_kernel, count, parts),
        grid_spec=pltpu.PrefetchScalarGridSpec(
            num_scalar_prefetch=1,
            grid=(columns // step,),
            in_specs=[whole] * len(gated)
            + [pl.BlockSpec((wide, step), lambda j, spots: (0, j))] * count,
            out_specs=pl.BlockSpec((tokens, step), lambda j, spots: (0, j)),
            scratch_shapes=[pltpu.VMEM((tokens, count * wide), jnp.bfloat16)],
        ),
        out_shape=jax.ShapeDtypeStruct((tokens, columns), kind),
        name="project",
    )(spots, *gated, *pieces)


def local(query_feat, key_feat, value_feat, short_filter, long_filter, direct_gain, out_weight):
    tokens, channels = query_feat.shape
    devices = lax.axis_size("seq")
    sides = lax.axis_size("ch")
    here = lax.axis_index("seq")
    place = lax.axis_index("ch")
    depth, columns = out_weight.shape
    pairs = long_filter.shape[0] // devices
    inner, outer = 4, devices // 8
    small = sides == 2 and outer == 2 and depth % 256 == 0
    if not small:
        return plain(query_feat, key_feat, value_feat, short_filter, long_filter, direct_gain, out_weight)
    parts = PARTS
    twin = here // inner % 2
    rank = here // (2 * inner) * inner + here % inner

    def swap(block, axis, mask):
        return lax.ppermute(block, axis, [(i ^ mask, i) for i in range(lax.axis_size(axis))])

    with jax.named_scope("edge"):
        last = slice(tokens - (TAPS - 1), None)
        edges = shifted(jnp.stack([query_feat[last], key_feat[last], value_feat[last]]), "seq", 1)

    with jax.named_scope("weights"):
        with jax.named_scope("wz"):
            far = swap(out_weight, "seq", 2 * inner)
        with jax.named_scope("wx"):
            near = swap(out_weight, "seq", 2)
        with jax.named_scope("wc"):
            mate = swap(out_weight, "seq", 1)
        with jax.named_scope("wzx"):
            far_near = swap(far, "seq", 2)
        with jax.named_scope("wzc"):
            far_mate = swap(far, "seq", 1)
        with jax.named_scope("wxc"):
            near_mate = swap(near, "seq", 1)
        with jax.named_scope("wzxc"):
            far_near_mate = swap(far_near, "seq", 1)
        pieces = [out_weight, mate, near, near_mate, far, far_mate, far_near, far_near_mate]
        masks = [0, 1, 2, 3, 2 * inner, 2 * inner + 1, 2 * inner + 2, 2 * inner + 3]
        spots = []
        for mask in masks:
            owner = here ^ mask
            spots.append((owner // (2 * inner) != place) * inner + owner % inner)
        spots = jnp.stack(spots).astype(jnp.int32)

    with jax.named_scope("filters"):
        sent = long_filter.astype(jnp.bfloat16)
        sent = sent.reshape(2, parts, outer, inner, pairs // parts, tokens).transpose(2, 0, 3, 1, 4, 5)
        taps = lax.all_to_all(sent.reshape(devices, pairs, tokens), "seq", split_axis=0, concat_axis=0, tiled=True)
        taps = taps.astype(jnp.float32).transpose(1, 0, 2)
        taps = taps.reshape(pairs, devices * tokens // LANES, LANES)
        gain = direct_gain.reshape(2, parts, devices // 2, 2 * pairs // parts)
        gain = lax.dynamic_index_in_dim(lax.dynamic_index_in_dim(gain, twin, 0, False), rank, 1, False)
        gain = jnp.broadcast_to(gain.reshape(2 * pairs, 1), (2 * pairs, LANES))

    half = channels // 2
    wide = depth
    with jax.named_scope("queries"):
        padded = jnp.pad(edges[0], ((0, PACK - (TAPS - 1)), (0, 0)))
        asked = jnp.concatenate([query_feat, padded], axis=0)
        asked = lax.dynamic_slice_in_dim(asked, (1 - twin) * half, half, 1)
        asked = swap(asked, "seq", inner)
        asked_edge = asked[tokens : tokens + TAPS - 1]

    def at(i):
        return (i // (2 * inner) * inner + i % inner) * 2 + i // inner % 2

    groups = [[o * 2 * inner + t * inner + i for o in range(outer) for i in range(inner)] for t in range(2)]
    spreads, backs = [], []
    for part in range(parts):
        with jax.named_scope(f"mix{part}"):
            turned = mix(key_feat, value_feat, edges, short_filter, part, parts, outer, inner)
            turned = turned.reshape(devices, 2 * pairs // parts, tokens)
        with jax.named_scope(f"spread{part}"):
            spreads.append(lax.all_to_all(turned, "seq", split_axis=0, concat_axis=0, tiled=True))
    for part in range(parts):
        with jax.named_scope(f"conv{part}"):
            conv = convolve(spreads[part], taps, gain, part, at)
            conv = conv.reshape(devices // 2, 2, 2 * pairs // parts, tokens)
        with jax.named_scope(f"back{part}"):
            backs.append(
                lax.all_to_all(conv, "seq", split_axis=0, concat_axis=0, tiled=True, axis_index_groups=groups)
            )
    blocks = half // wide
    kept_spot = jnp.stack([twin * blocks, twin * blocks, twin]).astype(jnp.int32)
    given_spot = jnp.stack([0 * twin, twin * blocks, 1 - twin]).astype(jnp.int32)
    kept, given = [], []
    for part in range(parts):
        with jax.named_scope(f"given{part}"):
            given.append(gate(given_spot, asked, asked_edge, short_filter, backs[part], part, wide))
        with jax.named_scope(f"kept{part}"):
            kept.append(gate(kept_spot, query_feat, edges[0], short_filter, backs[part], part, wide))
    given_far, kept_far = [], []
    for part in range(parts):
        with jax.named_scope(f"givenswap{part}"):
            given_far.append(swap(given[part], "ch", 1))
        with jax.named_scope(f"keptswap{part}"):
            kept_far.append(swap(kept[part], "ch", 1))
    with jax.named_scope("givenout"):
        sums = project(spots, given + given_far, pieces, parts, jnp.bfloat16)
    with jax.named_scope("outswap"):
        taken = swap(sums, "seq", inner)
    with jax.named_scope("keptout"):
        sums = project(spots, kept + kept_far, pieces, parts, jnp.float32)
    return (sums + taken.astype(jnp.float32)).astype(jnp.bfloat16)


def solution(mesh):
    in_specs = (
        P("seq", "ch"),
        P("seq", "ch"),
        P("seq", "ch"),
        P(None, None, "ch"),
        P("ch", "seq"),
        P("ch"),
        P("seq", "ch"),
    )
    return jax.shard_map(
        local, mesh=mesh, in_specs=in_specs, out_specs=P("seq", "ch"), check_vma=False
    )
```

```python
import functools

import jax
import jax.numpy as jnp
from jax import lax
from jax.experimental import pallas as pl
from jax.experimental.pallas import tpu as pltpu
from jax.sharding import PartitionSpec as P


TAPS = 3
PARTS = 2
LANES = 128
PACK = 16


def shifted(block, axis, distance):
    devices = range(lax.axis_size(axis))
    route = [(i - distance, i) for i in devices if i - distance in devices]
    return lax.ppermute(block, axis, route)


def featurized(inputs, edge, taps):
    rows = inputs.astype(jnp.float32)
    index = lax.broadcasted_iota(jnp.int32, rows.shape, 0)
    total = taps[0:1] * rows
    for tap in range(1, TAPS):
        moved = pltpu.roll(rows, tap, 0)
        for row in range(tap):
            first = TAPS - 1 - tap + row
            moved = jnp.where(index == row, edge[first : first + 1], moved)
        total = total + taps[tap : tap + 1] * moved
    return total


def mix_kernel(key_ref, value_ref, edge_ref, short_ref, turned_ref):
    edge = edge_ref[...].astype(jnp.float32)
    mixed = featurized(key_ref[...], edge[1], short_ref[1]) * featurized(
        value_ref[...], edge[2], short_ref[2]
    )
    turned_ref[...] = mixed.T.astype(jnp.bfloat16).reshape(turned_ref.shape)


def gate_kernel(query_ref, edge_ref, short_ref, conv_ref, gated_ref):
    edge = edge_ref[...].astype(jnp.float32)
    query_short = featurized(query_ref[...], edge, short_ref[0])
    summed = conv_ref[...].astype(jnp.float32).reshape(query_short.shape[1], query_short.shape[0]).T
    gated_ref[0] = (query_short * summed).astype(jnp.bfloat16)


def conv_kernel(n, tok, width, place, x_ref, f_ref, gain_ref, y_ref, xi, xs, ys):
    halves = tok // LANES
    groups = LANES // PACK
    for e in range(halves):
        for i in range(n):
            xi[e, i * width : (i + 1) * width, :] = x_ref[
                i, :, e * LANES : (e + 1) * LANES
            ].astype(jnp.float32)
        for c in range(width):
            xs[e, c, 0:n, :] = jnp.zeros((n, LANES), jnp.float32)
            xs[e, c, n : 2 * n, :] = xi[e, pl.ds(c, n, stride=width), :]
    lane = lax.broadcasted_iota(jnp.int32, (PACK, LANES), 1)
    sub = lax.broadcasted_iota(jnp.int32, (PACK, LANES), 0)

    def one(p, carry):
        def skewed(m):
            if m == 0:
                return jnp.zeros((PACK, LANES), jnp.float32)
            row = f_ref[p, m - 1 : m, :]
            return pltpu.roll(
                jnp.broadcast_to(row, (PACK, LANES)), 0, 1, stride=1, stride_axis=0
            )

        def turns(m, part):
            now = skewed(m)
            base = jnp.where(lane >= sub, now, part).astype(jnp.bfloat16)
            return now, [base] + [
                pltpu.roll(base, LANES - PACK * k, 1) for k in range(1, groups)
            ]

        def stack(before, after):
            tiles = [after[0]]
            for k in range(groups - 1, 0, -1):
                tiles.append(jnp.where(lane < LANES - PACK * k, before[k], after[k]))
            return jnp.concatenate(tiles, axis=0)

        part, before = turns(0, skewed(0))
        old = jnp.zeros((LANES, LANES), jnp.bfloat16)
        acc = None
        for d in range(n):
            cols = [old]
            for e in range(halves):
                part, after = turns(d * halves + e + 1, part)
                cols.append(stack(before, after))
                before = after
            old = cols[-1]
            rhs = jnp.concatenate(
                [jnp.concatenate(cols[1:], axis=1), jnp.concatenate(cols[:-1], axis=1)], axis=0
            )
            lhs = jnp.concatenate(
                [
                    jnp.concatenate(
                        [
                            xs[e, 2 * p + c, n - d : 2 * n - d, :].astype(jnp.bfloat16)
                            for e in range(halves)
                        ],
                        axis=1,
                    )
                    for c in range(2)
                ],
                axis=0,
            )
            out = jnp.dot(lhs, rhs, preferred_element_type=jnp.float32)
            acc = out if acc is None else acc + out
        for e in range(halves):
            for c in range(2):
                ys[e, pl.ds(2 * p + c, n, stride=width), :] = acc[
                    c * n : (c + 1) * n, e * LANES : (e + 1) * LANES
                ]
        return carry

    lax.fori_loop(0, width // 2, one, 0, unroll=4 if n <= 16 else 1)
    for e in range(halves):
        for i in range(n):
            rows = slice(i * width, (i + 1) * width)
            total = ys[e, rows, :] + gain_ref[...] * xi[e, rows, :]
            y_ref[place(i), :, e * LANES : (e + 1) * LANES] = total.astype(jnp.bfloat16)


def convolve(x, f, gain, part, place):
    n, chans, tok = x.shape
    width = min(16, chans)
    halves = tok // LANES
    assert halves == 2
    return pl.pallas_call(
        functools.partial(conv_kernel, n, tok, width, place),
        grid=(chans // width,),
        in_specs=[
            pl.BlockSpec((n, width, tok), lambda g: (0, g, 0)),
            pl.BlockSpec(
                (width // 2, n * halves, LANES), lambda g: (g + part * (chans // width), 0, 0)
            ),
            pl.BlockSpec((width, LANES), lambda g: (g + part * (chans // width), 0)),
        ],
        out_specs=pl.BlockSpec((n, width, tok), lambda g: (0, g, 0)),
        out_shape=jax.ShapeDtypeStruct(x.shape, jnp.bfloat16),
        scratch_shapes=[
            pltpu.VMEM((halves, n * width, LANES), jnp.float32),
            pltpu.VMEM((halves, width, 2 * n, LANES), jnp.float32),
            pltpu.VMEM((halves, n * width, LANES), jnp.float32),
        ],
        name="convolve",
    )(x, f, gain)


def mix(key_feat, value_feat, edges, short_filter, part, parts, outer, inner):
    tokens, channels = key_feat.shape
    wide = channels // (2 * parts)
    return pl.pallas_call(
        mix_kernel,
        grid=(2,),
        in_specs=[
            pl.BlockSpec((tokens, wide), lambda g: (0, g * parts + part)),
            pl.BlockSpec((tokens, wide), lambda g: (0, g * parts + part)),
            pl.BlockSpec((3, TAPS - 1, wide), lambda g: (0, 0, g * parts + part)),
            pl.BlockSpec((3, TAPS, wide), lambda g: (0, 0, g * parts + part)),
        ],
        out_specs=pl.BlockSpec(
            (outer, 1, inner, wide // (outer * inner), tokens), lambda g: (0, g, 0, 0, 0)
        ),
        out_shape=jax.ShapeDtypeStruct(
            (outer, 2, inner, wide // (outer * inner), tokens), jnp.bfloat16
        ),
        name="mix",
    )(key_feat, value_feat, edges, short_filter)


def gate(spot, query, edge, short_filter, conv, first, wide):
    sources, _, each, tokens = conv.shape
    blocks = sources * each // wide
    per = wide // each
    return pl.pallas_call(
        lambda spot_ref, *refs: gate_kernel(*refs),
        grid_spec=pltpu.PrefetchScalarGridSpec(
            num_scalar_prefetch=1,
            grid=(blocks,),
            in_specs=[
                pl.BlockSpec((tokens, wide), lambda g, spot: (0, spot[0] + g + first * blocks)),
                pl.BlockSpec((TAPS - 1, wide), lambda g, spot: (0, spot[0] + g + first * blocks)),
                pl.BlockSpec((3, TAPS, wide), lambda g, spot: (0, 0, spot[1] + g + first * blocks)),
                pl.BlockSpec((per, 1, each, tokens), lambda g, spot: (g, spot[2], 0, 0)),
            ],
            out_specs=pl.BlockSpec((1, tokens, wide), lambda g, spot: (g, 0, 0)),
        ),
        out_shape=jax.ShapeDtypeStruct((blocks, tokens, wide), jnp.bfloat16),
        name="gate",
    )(spot, query, edge, short_filter, conv)


def plain(query_feat, key_feat, value_feat, short_filter, long_filter, direct_gain, out_weight):
    tokens, channels = query_feat.shape
    devices = lax.axis_size("seq")
    pairs = long_filter.shape[0] // devices
    here = lax.axis_index("seq")
    weights = lax.all_gather(out_weight, "seq", axis=0, tiled=True)
    last = slice(tokens - (TAPS - 1), None)
    edges = shifted(jnp.stack([query_feat[last], key_feat[last], value_feat[last]]), "seq", 1)
    sent = long_filter.astype(jnp.bfloat16).reshape(devices, pairs, tokens)
    taps = lax.all_to_all(sent, "seq", split_axis=0, concat_axis=0, tiled=True)
    taps = taps.astype(jnp.float32).transpose(1, 0, 2)
    taps = taps.reshape(pairs, devices * tokens // LANES, LANES)
    gain = lax.dynamic_index_in_dim(direct_gain.reshape(devices, 2 * pairs, 1), here, 0, False)
    gain = jnp.broadcast_to(gain, (2 * pairs, LANES))
    turned = mix(key_feat, value_feat, edges, short_filter, 0, 1, 1, devices // 2)
    turned = turned.reshape(devices, 2 * pairs, tokens)
    spread = lax.all_to_all(turned, "seq", split_axis=0, concat_axis=0, tiled=True)
    conv = convolve(spread, taps, gain, 0, lambda i: i)
    conv = lax.all_to_all(conv, "seq", split_axis=0, concat_axis=0, tiled=True)
    wide = min(256, channels)
    spot = jnp.zeros((3,), jnp.int32)
    gated = gate(spot, query_feat, edges[0], short_filter, conv[:, None], 0, wide)
    gated = gated.transpose(1, 0, 2).reshape(tokens, channels)
    features = lax.all_gather(gated, "ch", axis=1, tiled=True)
    return jnp.dot(features, weights, preferred_element_type=jnp.float32).astype(jnp.bfloat16)


def project_kernel(count, parts, spots, *refs):
    gated, pieces = refs[: 2 * parts], refs[2 * parts : 2 * parts + count]
    out_ref, rows = refs[2 * parts + count :]
    blocks, _, wide = gated[0].shape

    @pl.when(pl.program_id(0) == 0)
    def _():
        for piece in range(count):
            spot = spots[piece]
            for source in range(2 * parts):

                @pl.when(spot // blocks == source)
                def _():
                    rows[:, piece * wide : (piece + 1) * wide] = gated[source][lax.rem(spot, blocks)]

    total = None
    for piece in range(count):
        out = jnp.dot(
            rows[:, piece * wide : (piece + 1) * wide],
            pieces[piece][...],
            preferred_element_type=jnp.float32,
        )
        total = out if total is None else total + out
    out_ref[...] = total.astype(out_ref.dtype)


def project(spots, gated, pieces, parts, kind):
    blocks, tokens, wide = gated[0].shape
    count = len(pieces)
    columns = pieces[0].shape[1]
    step = min(512, columns)
    whole = pl.BlockSpec((blocks, tokens, wide), lambda j, spots: (0, 0, 0))
    return pl.pallas_call(
        functools.partial(project_kernel, count, parts),
        grid_spec=pltpu.PrefetchScalarGridSpec(
            num_scalar_prefetch=1,
            grid=(columns // step,),
            in_specs=[whole] * len(gated)
            + [pl.BlockSpec((wide, step), lambda j, spots: (0, j))] * count,
            out_specs=pl.BlockSpec((tokens, step), lambda j, spots: (0, j)),
            scratch_shapes=[pltpu.VMEM((tokens, count * wide), jnp.bfloat16)],
        ),
        out_shape=jax.ShapeDtypeStruct((tokens, columns), kind),
        name="project",
    )(spots, *gated, *pieces)


def layer(query_feat, key_feat, value_feat, short_filter, long_filter, direct_gain, out_weight):
    tokens, channels = query_feat.shape
    devices = lax.axis_size("seq")
    sides = lax.axis_size("ch")
    here = lax.axis_index("seq")
    place = lax.axis_index("ch")
    depth, _ = out_weight.shape
    pairs = long_filter.shape[0] // devices
    inner, outer = 4, devices // 8
    small = sides == 2 and outer == 2 and depth % 256 == 0
    if not small:
        return plain(query_feat, key_feat, value_feat, short_filter, long_filter, direct_gain, out_weight)
    parts = PARTS
    twin = here // inner % 2
    rank = here // (2 * inner) * inner + here % inner

    def swap(block, axis, mask):
        return lax.ppermute(block, axis, [(i ^ mask, i) for i in range(lax.axis_size(axis))])

    last = slice(tokens - (TAPS - 1), None)
    edges = shifted(jnp.stack([query_feat[last], key_feat[last], value_feat[last]]), "seq", 1)

    far = swap(out_weight, "seq", 2 * inner)
    near = swap(out_weight, "seq", 2)
    mate = swap(out_weight, "seq", 1)
    far_near = swap(far, "seq", 2)
    far_mate = swap(far, "seq", 1)
    near_mate = swap(near, "seq", 1)
    far_near_mate = swap(far_near, "seq", 1)
    pieces = [out_weight, mate, near, near_mate, far, far_mate, far_near, far_near_mate]
    masks = [0, 1, 2, 3, 2 * inner, 2 * inner + 1, 2 * inner + 2, 2 * inner + 3]
    spots = []
    for mask in masks:
        owner = here ^ mask
        spots.append((owner // (2 * inner) != place) * inner + owner % inner)
    spots = jnp.stack(spots).astype(jnp.int32)

    sent = long_filter.astype(jnp.bfloat16)
    sent = sent.reshape(2, parts, outer, inner, pairs // parts, tokens).transpose(2, 0, 3, 1, 4, 5)
    taps = lax.all_to_all(sent.reshape(devices, pairs, tokens), "seq", split_axis=0, concat_axis=0, tiled=True)
    taps = taps.astype(jnp.float32).transpose(1, 0, 2)
    taps = taps.reshape(pairs, devices * tokens // LANES, LANES)
    gain = direct_gain.reshape(2, parts, devices // 2, 2 * pairs // parts)
    gain = lax.dynamic_index_in_dim(lax.dynamic_index_in_dim(gain, twin, 0, False), rank, 1, False)
    gain = jnp.broadcast_to(gain.reshape(2 * pairs, 1), (2 * pairs, LANES))

    half = channels // 2
    wide = depth
    padded = jnp.pad(edges[0], ((0, PACK - (TAPS - 1)), (0, 0)))
    asked = jnp.concatenate([query_feat, padded], axis=0)
    asked = lax.dynamic_slice_in_dim(asked, (1 - twin) * half, half, 1)
    asked = swap(asked, "seq", inner)
    asked_edge = asked[tokens : tokens + TAPS - 1]

    def at(i):
        return (i // (2 * inner) * inner + i % inner) * 2 + i // inner % 2

    groups = [[o * 2 * inner + t * inner + i for o in range(outer) for i in range(inner)] for t in range(2)]
    spreads, backs = [], []
    for part in range(parts):
        turned = mix(key_feat, value_feat, edges, short_filter, part, parts, outer, inner)
        turned = turned.reshape(devices, 2 * pairs // parts, tokens)
        spreads.append(lax.all_to_all(turned, "seq", split_axis=0, concat_axis=0, tiled=True))
    for part in range(parts):
        conv = convolve(spreads[part], taps, gain, part, at)
        conv = conv.reshape(devices // 2, 2, 2 * pairs // parts, tokens)
        backs.append(
            lax.all_to_all(conv, "seq", split_axis=0, concat_axis=0, tiled=True, axis_index_groups=groups)
        )
    blocks = half // wide
    kept_spot = jnp.stack([twin * blocks, twin * blocks, twin]).astype(jnp.int32)
    given_spot = jnp.stack([0 * twin, twin * blocks, 1 - twin]).astype(jnp.int32)
    kept, given = [], []
    for part in range(parts):
        given.append(gate(given_spot, asked, asked_edge, short_filter, backs[part], part, wide))
        kept.append(gate(kept_spot, query_feat, edges[0], short_filter, backs[part], part, wide))
    given_far, kept_far = [], []
    for part in range(parts):
        given_far.append(swap(given[part], "ch", 1))
        kept_far.append(swap(kept[part], "ch", 1))
    sums = project(spots, given + given_far, pieces, parts, jnp.bfloat16)
    taken = swap(sums, "seq", inner)
    sums = project(spots, kept + kept_far, pieces, parts, jnp.float32)
    return (sums + taken.astype(jnp.float32)).astype(jnp.bfloat16)


def solution(mesh):
    in_specs = (
        P("seq", "ch"),
        P("seq", "ch"),
        P("seq", "ch"),
        P(None, None, "ch"),
        P("ch", "seq"),
        P("ch"),
        P("seq", "ch"),
    )
    return jax.shard_map(layer, mesh=mesh, in_specs=in_specs, out_specs=P("seq", "ch"), check_vma=False)
```

```python
import functools

import jax
import jax.numpy as jnp
from jax import lax
from jax.experimental import pallas as pl
from jax.experimental.pallas import tpu as pltpu
from jax.sharding import PartitionSpec as P


TAPS = 3
PARTS = 2
CUTS = 2
LANES = 128
PACK = 16


def shifted(block, axis, distance):
    devices = range(lax.axis_size(axis))
    route = [(i - distance, i) for i in devices if i - distance in devices]
    return lax.ppermute(block, axis, route)


def featurized(inputs, edge, taps):
    rows = inputs.astype(jnp.float32)
    index = lax.broadcasted_iota(jnp.int32, rows.shape, 0)
    total = taps[0:1] * rows
    for tap in range(1, TAPS):
        moved = pltpu.roll(rows, tap, 0)
        for row in range(tap):
            first = TAPS - 1 - tap + row
            moved = jnp.where(index == row, edge[first : first + 1], moved)
        total = total + taps[tap : tap + 1] * moved
    return total


def mix_kernel(key_ref, value_ref, edge_ref, short_ref, turned_ref):
    edge = edge_ref[...].astype(jnp.float32)
    mixed = featurized(key_ref[...], edge[1], short_ref[1]) * featurized(
        value_ref[...], edge[2], short_ref[2]
    )
    turned_ref[...] = mixed.T.astype(jnp.bfloat16).reshape(turned_ref.shape)


def gate_kernel(query_ref, edge_ref, short_ref, conv_ref, gated_ref):
    edge = edge_ref[...].astype(jnp.float32)
    query_short = featurized(query_ref[...], edge, short_ref[0])
    summed = conv_ref[...].astype(jnp.float32).reshape(query_short.shape[1], query_short.shape[0]).T
    gated_ref[0] = (query_short * summed).astype(jnp.bfloat16)


def conv_kernel(n, tok, width, place, x_ref, f_ref, gain_ref, y_ref, xi, xs, ys):
    halves = tok // LANES
    groups = LANES // PACK
    for e in range(halves):
        for i in range(n):
            xi[e, i * width : (i + 1) * width, :] = x_ref[
                i, :, e * LANES : (e + 1) * LANES
            ].astype(jnp.float32)
        for c in range(width):
            xs[e, c, 0:n, :] = jnp.zeros((n, LANES), jnp.float32)
            xs[e, c, n : 2 * n, :] = xi[e, pl.ds(c, n, stride=width), :]
    lane = lax.broadcasted_iota(jnp.int32, (PACK, LANES), 1)
    sub = lax.broadcasted_iota(jnp.int32, (PACK, LANES), 0)

    def one(p, carry):
        def skewed(m):
            if m == 0:
                return jnp.zeros((PACK, LANES), jnp.float32)
            row = f_ref[p, m - 1 : m, :]
            return pltpu.roll(
                jnp.broadcast_to(row, (PACK, LANES)), 0, 1, stride=1, stride_axis=0
            )

        def turns(m, part):
            now = skewed(m)
            base = jnp.where(lane >= sub, now, part).astype(jnp.bfloat16)
            return now, [base] + [
                pltpu.roll(base, LANES - PACK * k, 1) for k in range(1, groups)
            ]

        def stack(before, after):
            tiles = [after[0]]
            for k in range(groups - 1, 0, -1):
                tiles.append(jnp.where(lane < LANES - PACK * k, before[k], after[k]))
            return jnp.concatenate(tiles, axis=0)

        part, before = turns(0, skewed(0))
        old = jnp.zeros((LANES, LANES), jnp.bfloat16)
        acc = None
        for d in range(n):
            cols = [old]
            for e in range(halves):
                part, after = turns(d * halves + e + 1, part)
                cols.append(stack(before, after))
                before = after
            old = cols[-1]
            rhs = jnp.concatenate(
                [jnp.concatenate(cols[1:], axis=1), jnp.concatenate(cols[:-1], axis=1)], axis=0
            )
            lhs = jnp.concatenate(
                [
                    jnp.concatenate(
                        [
                            xs[e, 2 * p + c, n - d : 2 * n - d, :].astype(jnp.bfloat16)
                            for e in range(halves)
                        ],
                        axis=1,
                    )
                    for c in range(2)
                ],
                axis=0,
            )
            out = jnp.dot(lhs, rhs, preferred_element_type=jnp.float32)
            acc = out if acc is None else acc + out
        for e in range(halves):
            for c in range(2):
                ys[e, pl.ds(2 * p + c, n, stride=width), :] = acc[
                    c * n : (c + 1) * n, e * LANES : (e + 1) * LANES
                ]
        return carry

    lax.fori_loop(0, width // 2, one, 0, unroll=4 if n <= 16 else 1)
    for e in range(halves):
        for i in range(n):
            rows = slice(i * width, (i + 1) * width)
            total = ys[e, rows, :] + gain_ref[...] * xi[e, rows, :]
            y_ref[place(i), :, e * LANES : (e + 1) * LANES] = total.astype(jnp.bfloat16)


def convolve(x, f, gain, part, place):
    n, chans, tok = x.shape
    width = min(16, chans)
    halves = tok // LANES
    assert halves == 2
    return pl.pallas_call(
        functools.partial(conv_kernel, n, tok, width, place),
        grid=(chans // width,),
        in_specs=[
            pl.BlockSpec((n, width, tok), lambda g: (0, g, 0)),
            pl.BlockSpec(
                (width // 2, n * halves, LANES), lambda g: (g + part * (chans // width), 0, 0)
            ),
            pl.BlockSpec((width, LANES), lambda g: (g + part * (chans // width), 0)),
        ],
        out_specs=pl.BlockSpec((n, width, tok), lambda g: (0, g, 0)),
        out_shape=jax.ShapeDtypeStruct(x.shape, jnp.bfloat16),
        scratch_shapes=[
            pltpu.VMEM((halves, n * width, LANES), jnp.float32),
            pltpu.VMEM((halves, width, 2 * n, LANES), jnp.float32),
            pltpu.VMEM((halves, n * width, LANES), jnp.float32),
        ],
        name="convolve",
    )(x, f, gain)


def mix(key_feat, value_feat, edges, short_filter, part, parts, outer, inner):
    tokens, channels = key_feat.shape
    wide = channels // (2 * parts)
    return pl.pallas_call(
        mix_kernel,
        grid=(2,),
        in_specs=[
            pl.BlockSpec((tokens, wide), lambda g: (0, g * parts + part)),
            pl.BlockSpec((tokens, wide), lambda g: (0, g * parts + part)),
            pl.BlockSpec((3, TAPS - 1, wide), lambda g: (0, 0, g * parts + part)),
            pl.BlockSpec((3, TAPS, wide), lambda g: (0, 0, g * parts + part)),
        ],
        out_specs=pl.BlockSpec(
            (outer, 1, inner, wide // (outer * inner), tokens), lambda g: (0, g, 0, 0, 0)
        ),
        out_shape=jax.ShapeDtypeStruct(
            (outer, 2, inner, wide // (outer * inner), tokens), jnp.bfloat16
        ),
        name="mix",
    )(key_feat, value_feat, edges, short_filter)


def gate(spot, query, edge, short_filter, conv, first, wide):
    sources, _, each, tokens = conv.shape
    blocks = sources * each // wide
    per = wide // each
    return pl.pallas_call(
        lambda spot_ref, *refs: gate_kernel(*refs),
        grid_spec=pltpu.PrefetchScalarGridSpec(
            num_scalar_prefetch=1,
            grid=(blocks,),
            in_specs=[
                pl.BlockSpec((tokens, wide), lambda g, spot: (0, spot[0] + g + first * blocks)),
                pl.BlockSpec((TAPS - 1, wide), lambda g, spot: (0, spot[0] + g + first * blocks)),
                pl.BlockSpec((3, TAPS, wide), lambda g, spot: (0, 0, spot[1] + g + first * blocks)),
                pl.BlockSpec((per, 1, each, tokens), lambda g, spot: (g, spot[2], 0, 0)),
            ],
            out_specs=pl.BlockSpec((1, tokens, wide), lambda g, spot: (g, 0, 0)),
        ),
        out_shape=jax.ShapeDtypeStruct((blocks, tokens, wide), jnp.bfloat16),
        name="gate",
    )(spot, query, edge, short_filter, conv)


def plain(query_feat, key_feat, value_feat, short_filter, long_filter, direct_gain, out_weight):
    tokens, channels = query_feat.shape
    devices = lax.axis_size("seq")
    pairs = long_filter.shape[0] // devices
    here = lax.axis_index("seq")
    weights = lax.all_gather(out_weight, "seq", axis=0, tiled=True)
    last = slice(tokens - (TAPS - 1), None)
    edges = shifted(jnp.stack([query_feat[last], key_feat[last], value_feat[last]]), "seq", 1)
    sent = long_filter.astype(jnp.bfloat16).reshape(devices, pairs, tokens)
    taps = lax.all_to_all(sent, "seq", split_axis=0, concat_axis=0, tiled=True)
    taps = taps.astype(jnp.float32).transpose(1, 0, 2)
    taps = taps.reshape(pairs, devices * tokens // LANES, LANES)
    gain = lax.dynamic_index_in_dim(direct_gain.reshape(devices, 2 * pairs, 1), here, 0, False)
    gain = jnp.broadcast_to(gain, (2 * pairs, LANES))
    turned = mix(key_feat, value_feat, edges, short_filter, 0, 1, 1, devices // 2)
    turned = turned.reshape(devices, 2 * pairs, tokens)
    spread = lax.all_to_all(turned, "seq", split_axis=0, concat_axis=0, tiled=True)
    conv = convolve(spread, taps, gain, 0, lambda i: i)
    conv = lax.all_to_all(conv, "seq", split_axis=0, concat_axis=0, tiled=True)
    wide = min(256, channels)
    spot = jnp.zeros((3,), jnp.int32)
    gated = gate(spot, query_feat, edges[0], short_filter, conv[:, None], 0, wide)
    gated = gated.transpose(1, 0, 2).reshape(tokens, channels)
    features = lax.all_gather(gated, "ch", axis=1, tiled=True)
    return jnp.dot(features, weights, preferred_element_type=jnp.float32).astype(jnp.bfloat16)


def project_kernel(count, parts, spots, *refs):
    gated, pieces = refs[: 2 * parts], refs[2 * parts : 2 * parts + count]
    out_ref, rows = refs[2 * parts + count :]
    blocks, _, wide = gated[0].shape

    @pl.when(pl.program_id(0) == 0)
    def _():
        for piece in range(count):
            spot = spots[piece]
            for source in range(2 * parts):

                @pl.when(spot // blocks == source)
                def _():
                    rows[:, piece * wide : (piece + 1) * wide] = gated[source][lax.rem(spot, blocks)]

    total = None
    for piece in range(count):
        out = jnp.dot(
            rows[:, piece * wide : (piece + 1) * wide],
            pieces[piece][...],
            preferred_element_type=jnp.float32,
        )
        total = out if total is None else total + out
    out_ref[...] = total.astype(out_ref.dtype)


def project(spots, gated, pieces, parts, kind, columns, first):
    blocks, tokens, wide = gated[0].shape
    count = len(pieces)
    step = min(512, columns)

    def held(piece):
        skip = first // step if piece.shape[1] > columns else 0
        return pl.BlockSpec((wide, step), lambda j, spots: (0, j + skip))

    whole = pl.BlockSpec((blocks, tokens, wide), lambda j, spots: (0, 0, 0))
    return pl.pallas_call(
        functools.partial(project_kernel, count, parts),
        grid_spec=pltpu.PrefetchScalarGridSpec(
            num_scalar_prefetch=1,
            grid=(columns // step,),
            in_specs=[whole] * len(gated)
            + [held(piece) for piece in pieces],
            out_specs=pl.BlockSpec((tokens, step), lambda j, spots: (0, j)),
            scratch_shapes=[pltpu.VMEM((tokens, count * wide), jnp.bfloat16)],
        ),
        out_shape=jax.ShapeDtypeStruct((tokens, columns), kind),
        name="project",
    )(spots, *gated, *pieces)


def layer(query_feat, key_feat, value_feat, short_filter, long_filter, direct_gain, out_weight):
    tokens, channels = query_feat.shape
    devices = lax.axis_size("seq")
    sides = lax.axis_size("ch")
    here = lax.axis_index("seq")
    place = lax.axis_index("ch")
    depth, columns = out_weight.shape
    pairs = long_filter.shape[0] // devices
    inner, outer = 4, devices // 8
    small = sides == 2 and outer == 2 and depth % 256 == 0
    if not small:
        return plain(query_feat, key_feat, value_feat, short_filter, long_filter, direct_gain, out_weight)
    parts = PARTS
    twin = here // inner % 2
    rank = here // (2 * inner) * inner + here % inner

    def swap(block, axis, mask):
        return lax.ppermute(block, axis, [(i ^ mask, i) for i in range(lax.axis_size(axis))])

    last = slice(tokens - (TAPS - 1), None)
    edges = shifted(jnp.stack([query_feat[last], key_feat[last], value_feat[last]]), "seq", 1)

    near = swap(out_weight, "seq", 2)
    mate = swap(out_weight, "seq", 1)
    near_mate = swap(near, "seq", 1)
    span = columns // CUTS
    pieces = []
    for cut in range(CUTS):
        far = swap(out_weight[:, cut * span : (cut + 1) * span], "seq", 2 * inner)
        far_near = swap(far, "seq", 2)
        far_mate = swap(far, "seq", 1)
        far_near_mate = swap(far_near, "seq", 1)
        pieces.append(
            [out_weight, mate, near, near_mate, far, far_mate, far_near, far_near_mate]
        )
    masks = [0, 1, 2, 3, 2 * inner, 2 * inner + 1, 2 * inner + 2, 2 * inner + 3]
    spots = []
    for mask in masks:
        owner = here ^ mask
        spots.append((owner // (2 * inner) != place) * inner + owner % inner)
    spots = jnp.stack(spots).astype(jnp.int32)

    sent = long_filter.astype(jnp.bfloat16)
    sent = sent.reshape(2, parts, outer, inner, pairs // parts, tokens).transpose(2, 0, 3, 1, 4, 5)
    taps = lax.all_to_all(sent.reshape(devices, pairs, tokens), "seq", split_axis=0, concat_axis=0, tiled=True)
    taps = taps.astype(jnp.float32).transpose(1, 0, 2)
    taps = taps.reshape(pairs, devices * tokens // LANES, LANES)
    gain = direct_gain.reshape(2, parts, devices // 2, 2 * pairs // parts)
    gain = lax.dynamic_index_in_dim(lax.dynamic_index_in_dim(gain, twin, 0, False), rank, 1, False)
    gain = jnp.broadcast_to(gain.reshape(2 * pairs, 1), (2 * pairs, LANES))

    half = channels // 2
    wide = depth
    padded = jnp.pad(edges[0], ((0, PACK - (TAPS - 1)), (0, 0)))
    asked = jnp.concatenate([query_feat, padded], axis=0)
    asked = lax.dynamic_slice_in_dim(asked, (1 - twin) * half, half, 1)
    asked = swap(asked, "seq", inner)
    asked_edge = asked[tokens : tokens + TAPS - 1]

    def at(i):
        return (i // (2 * inner) * inner + i % inner) * 2 + i // inner % 2

    groups = [[o * 2 * inner + t * inner + i for o in range(outer) for i in range(inner)] for t in range(2)]
    spreads, backs = [], []
    for part in range(parts):
        turned = mix(key_feat, value_feat, edges, short_filter, part, parts, outer, inner)
        turned = turned.reshape(devices, 2 * pairs // parts, tokens)
        spreads.append(lax.all_to_all(turned, "seq", split_axis=0, concat_axis=0, tiled=True))
    for part in range(parts):
        conv = convolve(spreads[part], taps, gain, part, at)
        conv = conv.reshape(devices // 2, 2, 2 * pairs // parts, tokens)
        backs.append(
            lax.all_to_all(conv, "seq", split_axis=0, concat_axis=0, tiled=True, axis_index_groups=groups)
        )
    blocks = half // wide
    kept_spot = jnp.stack([twin * blocks, twin * blocks, twin]).astype(jnp.int32)
    given_spot = jnp.stack([0 * twin, twin * blocks, 1 - twin]).astype(jnp.int32)
    kept, given = [], []
    for part in range(parts):
        given.append(gate(given_spot, asked, asked_edge, short_filter, backs[part], part, wide))
        kept.append(gate(kept_spot, query_feat, edges[0], short_filter, backs[part], part, wide))
    given_far, kept_far = [], []
    for part in range(parts):
        given_far.append(swap(given[part], "ch", 1))
        kept_far.append(swap(kept[part], "ch", 1))
    outs = []
    for cut in range(CUTS):
        sums = project(spots, given + given_far, pieces[cut], parts, jnp.bfloat16, span, cut * span)
        outs.append(swap(sums, "seq", inner))
    for cut in range(CUTS):
        sums = project(spots, kept + kept_far, pieces[cut], parts, jnp.float32, span, cut * span)
        outs[cut] = (sums + outs[cut].astype(jnp.float32)).astype(jnp.bfloat16)
    return jnp.concatenate(outs, axis=1)


def solution(mesh):
    in_specs = (
        P("seq", "ch"),
        P("seq", "ch"),
        P("seq", "ch"),
        P(None, None, "ch"),
        P("ch", "seq"),
        P("ch"),
        P("seq", "ch"),
    )
    return jax.shard_map(layer, mesh=mesh, in_specs=in_specs, out_specs=P("seq", "ch"), check_vma=False)
```

```python
import functools

import jax
import jax.numpy as jnp
from jax import lax
from jax.experimental import pallas as pl
from jax.experimental.pallas import tpu as pltpu
from jax.sharding import PartitionSpec as P


TAPS = 3
PARTS = 2
CUTS = 2
LANES = 128
PACK = 16


def shifted(block, axis, distance):
    devices = range(lax.axis_size(axis))
    route = [(i - distance, i) for i in devices if i - distance in devices]
    return lax.ppermute(block, axis, route)


def featurized(inputs, edge, taps):
    rows = inputs.astype(jnp.float32)
    index = lax.broadcasted_iota(jnp.int32, rows.shape, 0)
    total = taps[0:1] * rows
    for tap in range(1, TAPS):
        moved = pltpu.roll(rows, tap, 0)
        for row in range(tap):
            first = TAPS - 1 - tap + row
            moved = jnp.where(index == row, edge[first : first + 1], moved)
        total = total + taps[tap : tap + 1] * moved
    return total


def mix_kernel(key_ref, value_ref, edge_ref, short_ref, *refs):
    sent_ref = refs[-1]
    outer, _, inner, _, tokens = sent_ref.shape
    edge = edge_ref[...].astype(jnp.float32)
    mixed = featurized(key_ref[...], edge[1], short_ref[1]) * featurized(
        value_ref[...], edge[2], short_ref[2]
    )
    each = mixed.shape[1] // (outer * inner)
    turned = mixed.T.astype(jnp.bfloat16)
    sent_ref[:, 0, :, 0:each, :] = turned.reshape(outer, inner, each, tokens)
    for taps_ref in refs[:-1]:
        taps = taps_ref[...].astype(jnp.bfloat16)
        sent_ref[:, 0, :, each:, :] = taps.reshape(outer, inner, each // 2, tokens)


def gate_kernel(count, *refs):
    short_ref = refs[0]
    for own in range(count):
        query_ref, edge_ref, conv_ref = refs[1 + 3 * own : 4 + 3 * own]
        gated_ref = refs[1 + 3 * count + own]
        edge = edge_ref[...].astype(jnp.float32)
        query_short = featurized(query_ref[...], edge, short_ref[0])
        wide, tokens = query_short.shape[1], query_short.shape[0]
        summed = conv_ref[...].astype(jnp.float32).reshape(wide, tokens).T
        gated_ref[0] = (query_short * summed).astype(jnp.bfloat16)


def conv_kernel(n, tok, width, place, x_ref, f_ref, gain_ref, y_ref, xi, xs, ys, fs):
    halves = tok // LANES
    groups = LANES // PACK
    for e in range(halves):
        for i in range(n):
            fs[:, i * halves + e, :] = f_ref[i, :, e * LANES : (e + 1) * LANES].astype(jnp.float32)
            xi[e, i * width : (i + 1) * width, :] = x_ref[
                i, :, e * LANES : (e + 1) * LANES
            ].astype(jnp.float32)
        for c in range(width):
            xs[e, c, 0:n, :] = jnp.zeros((n, LANES), jnp.float32)
            xs[e, c, n : 2 * n, :] = xi[e, pl.ds(c, n, stride=width), :]
    lane = lax.broadcasted_iota(jnp.int32, (PACK, LANES), 1)
    sub = lax.broadcasted_iota(jnp.int32, (PACK, LANES), 0)

    def one(p, carry):
        def skewed(m):
            if m == 0:
                return jnp.zeros((PACK, LANES), jnp.float32)
            row = fs[p, m - 1 : m, :]
            return pltpu.roll(
                jnp.broadcast_to(row, (PACK, LANES)), 0, 1, stride=1, stride_axis=0
            )

        def turns(m, part):
            now = skewed(m)
            base = jnp.where(lane >= sub, now, part).astype(jnp.bfloat16)
            return now, [base] + [
                pltpu.roll(base, LANES - PACK * k, 1) for k in range(1, groups)
            ]

        def stack(before, after):
            tiles = [after[0]]
            for k in range(groups - 1, 0, -1):
                tiles.append(jnp.where(lane < LANES - PACK * k, before[k], after[k]))
            return jnp.concatenate(tiles, axis=0)

        part, before = turns(0, skewed(0))
        old = jnp.zeros((LANES, LANES), jnp.bfloat16)
        acc = None
        for d in range(n):
            cols = [old]
            for e in range(halves):
                part, after = turns(d * halves + e + 1, part)
                cols.append(stack(before, after))
                before = after
            old = cols[-1]
            rhs = jnp.concatenate(
                [jnp.concatenate(cols[1:], axis=1), jnp.concatenate(cols[:-1], axis=1)], axis=0
            )
            lhs = jnp.concatenate(
                [
                    jnp.concatenate(
                        [
                            xs[e, 2 * p + c, n - d : 2 * n - d, :].astype(jnp.bfloat16)
                            for e in range(halves)
                        ],
                        axis=1,
                    )
                    for c in range(2)
                ],
                axis=0,
            )
            out = jnp.dot(lhs, rhs, preferred_element_type=jnp.float32)
            acc = out if acc is None else acc + out
        for e in range(halves):
            for c in range(2):
                ys[e, pl.ds(2 * p + c, n, stride=width), :] = acc[
                    c * n : (c + 1) * n, e * LANES : (e + 1) * LANES
                ]
        return carry

    lax.fori_loop(0, width // 2, one, 0, unroll=4 if n <= 16 else 1)
    for e in range(halves):
        for i in range(n):
            rows = slice(i * width, (i + 1) * width)
            total = ys[e, rows, :] + gain_ref[...] * xi[e, rows, :]
            y_ref[place(i), :, e * LANES : (e + 1) * LANES] = total.astype(jnp.bfloat16)


def convolve(x, f, skip, chans, gain, part, place):
    n, _, tok = x.shape
    width = min(16, chans)
    halves = tok // LANES
    assert halves == 2
    return pl.pallas_call(
        functools.partial(conv_kernel, n, tok, width, place),
        grid=(chans // width,),
        in_specs=[
            pl.BlockSpec((n, width, tok), lambda g: (0, g, 0)),
            pl.BlockSpec((n, width // 2, tok), lambda g: (0, g + skip // (width // 2), 0)),
            pl.BlockSpec((width, LANES), lambda g: (g + part * (chans // width), 0)),
        ],
        out_specs=pl.BlockSpec((n, width, tok), lambda g: (0, g, 0)),
        out_shape=jax.ShapeDtypeStruct((n, chans, tok), jnp.bfloat16),
        scratch_shapes=[
            pltpu.VMEM((halves, n * width, LANES), jnp.float32),
            pltpu.VMEM((halves, width, 2 * n, LANES), jnp.float32),
            pltpu.VMEM((halves, n * width, LANES), jnp.float32),
            pltpu.VMEM((width // 2, n * halves, LANES), jnp.float32),
        ],
        name="convolve",
    )(x, f, gain)


def mix(key_feat, value_feat, edges, short_filter, part, parts, outer, inner, *taps):
    tokens, channels = key_feat.shape
    wide = channels // (2 * parts)
    each = wide // (outer * inner)
    each += each // 2 * len(taps)
    rows = pl.BlockSpec((tokens, wide), lambda g: (0, g * parts + part))
    return pl.pallas_call(
        mix_kernel,
        grid=(2,),
        in_specs=[
            rows,
            rows,
            pl.BlockSpec((3, TAPS - 1, wide), lambda g: (0, 0, g * parts + part)),
            pl.BlockSpec((3, TAPS, wide), lambda g: (0, 0, g * parts + part)),
        ]
        + [pl.BlockSpec((wide // 2, tokens), lambda g: (g * parts + part, 0))] * len(taps),
        out_specs=pl.BlockSpec((outer, 1, inner, each, tokens), lambda g: (0, g, 0, 0, 0)),
        out_shape=jax.ShapeDtypeStruct((outer, 2, inner, each, tokens), jnp.bfloat16),
        name="mix",
    )(key_feat, value_feat, edges, short_filter, *taps)


def gate(spot, short_filter, conv, first, wide, *sources):
    count = len(sources)
    origins, _, each, tokens = conv.shape
    blocks = origins * each // wide
    per = wide // each
    specs, operands = [], []
    for own, (query, edge) in enumerate(sources):
        column = lambda g, spot, own=own: (0, spot[1 + 2 * own] + g + first * blocks)
        specs += [
            pl.BlockSpec((tokens, wide), column),
            pl.BlockSpec((TAPS - 1, wide), column),
            pl.BlockSpec((per, 1, each, tokens), lambda g, spot, own=own: (g, spot[2 + 2 * own], 0, 0)),
        ]
        operands += [query, edge, conv]
    return pl.pallas_call(
        lambda spot_ref, *refs: gate_kernel(count, *refs),
        grid_spec=pltpu.PrefetchScalarGridSpec(
            num_scalar_prefetch=1,
            grid=(blocks,),
            in_specs=[pl.BlockSpec((3, TAPS, wide), lambda g, spot: (0, 0, spot[0] + g + first * blocks))] + specs,
            out_specs=[pl.BlockSpec((1, tokens, wide), lambda g, spot: (g, 0, 0))] * count,
        ),
        out_shape=[jax.ShapeDtypeStruct((blocks, tokens, wide), jnp.bfloat16)] * count,
        name="gate",
    )(spot, short_filter, *operands)


def plain(query_feat, key_feat, value_feat, short_filter, long_filter, direct_gain, out_weight):
    tokens, channels = query_feat.shape
    devices = lax.axis_size("seq")
    pairs = long_filter.shape[0] // devices
    here = lax.axis_index("seq")
    weights = lax.all_gather(out_weight, "seq", axis=0, tiled=True)
    last = slice(tokens - (TAPS - 1), None)
    edges = shifted(jnp.stack([query_feat[last], key_feat[last], value_feat[last]]), "seq", 1)
    sent = long_filter.astype(jnp.bfloat16).reshape(devices, pairs, tokens)
    taps = lax.all_to_all(sent, "seq", split_axis=0, concat_axis=0, tiled=True)
    gain = lax.dynamic_index_in_dim(direct_gain.reshape(devices, 2 * pairs, 1), here, 0, False)
    gain = jnp.broadcast_to(gain, (2 * pairs, LANES))
    turned = mix(key_feat, value_feat, edges, short_filter, 0, 1, 1, devices // 2)
    turned = turned.reshape(devices, 2 * pairs, tokens)
    spread = lax.all_to_all(turned, "seq", split_axis=0, concat_axis=0, tiled=True)
    conv = convolve(spread, taps, 0, 2 * pairs, gain, 0, lambda i: i)
    conv = lax.all_to_all(conv, "seq", split_axis=0, concat_axis=0, tiled=True)
    wide = min(256, channels)
    spot = jnp.zeros((3,), jnp.int32)
    (gated,) = gate(spot, short_filter, conv[:, None], 0, wide, (query_feat, edges[0]))
    gated = gated.transpose(1, 0, 2).reshape(tokens, channels)
    features = lax.all_gather(gated, "ch", axis=1, tiled=True)
    return jnp.dot(features, weights, preferred_element_type=jnp.float32).astype(jnp.bfloat16)


def project_kernel(count, per, spots, *refs):
    gated, pieces = refs[:per], refs[per : per + count]
    out_ref, rows = refs[per + count :]
    blocks, _, wide = gated[0].shape

    @pl.when(pl.program_id(0) == 0)
    def _():
        for piece in range(count):
            spot = spots[piece]
            for source in range(per):

                @pl.when(spot // blocks == source)
                def _():
                    rows[:, piece * wide : (piece + 1) * wide] = gated[source][lax.rem(spot, blocks)]

    total = None
    for piece in range(count):
        out = jnp.dot(
            rows[:, piece * wide : (piece + 1) * wide],
            pieces[piece][...],
            preferred_element_type=jnp.float32,
        )
        total = out if total is None else total + out
    out_ref[...] = total.astype(out_ref.dtype)


def project(spots, gated, pieces, kind, columns, first):
    blocks, tokens, wide = gated[0].shape
    count = len(pieces)
    step = min(256, columns)

    def held(piece):
        skip = first // step if piece.shape[1] > columns else 0
        return pl.BlockSpec((wide, step), lambda j, spots: (0, j + skip))

    whole = pl.BlockSpec((blocks, tokens, wide), lambda j, spots: (0, 0, 0))
    return pl.pallas_call(
        functools.partial(project_kernel, count, len(gated)),
        grid_spec=pltpu.PrefetchScalarGridSpec(
            num_scalar_prefetch=1,
            grid=(columns // step,),
            in_specs=[whole] * len(gated) + [held(piece) for piece in pieces],
            out_specs=pl.BlockSpec((tokens, step), lambda j, spots: (0, j)),
            scratch_shapes=[pltpu.VMEM((tokens, count * wide), jnp.bfloat16)],
        ),
        out_shape=jax.ShapeDtypeStruct((tokens, columns), kind),
        name="project",
    )(spots, *gated, *pieces)


def layer(query_feat, key_feat, value_feat, short_filter, long_filter, direct_gain, out_weight):
    tokens, channels = query_feat.shape
    devices = lax.axis_size("seq")
    sides = lax.axis_size("ch")
    here = lax.axis_index("seq")
    place = lax.axis_index("ch")
    depth, columns = out_weight.shape
    pairs = long_filter.shape[0] // devices
    inner, outer = 4, devices // 8
    small = sides == 2 and outer == 2 and depth % 256 == 0
    if not small:
        return plain(query_feat, key_feat, value_feat, short_filter, long_filter, direct_gain, out_weight)
    parts = PARTS
    twin = here // inner % 2
    rank = here // (2 * inner) * inner + here % inner

    def swap(block, axis, mask):
        return lax.ppermute(block, axis, [(i ^ mask, i) for i in range(lax.axis_size(axis))])

    last = slice(tokens - (TAPS - 1), None)
    edges = shifted(jnp.stack([query_feat[last], key_feat[last], value_feat[last]]), "seq", 1)

    near = swap(out_weight, "seq", 2)
    mate = swap(out_weight, "seq", 1)
    near_mate = swap(near, "seq", 1)
    span = columns // CUTS
    pieces = []
    for cut in range(CUTS):
        far = swap(out_weight[:, cut * span : (cut + 1) * span], "seq", 2 * inner)
        far_near = swap(far, "seq", 2)
        far_mate = swap(far, "seq", 1)
        far_near_mate = swap(far_near, "seq", 1)
        pieces.append(
            [out_weight, mate, near, near_mate, far, far_mate, far_near, far_near_mate]
        )
    masks = [0, 1, 2, 3, 2 * inner, 2 * inner + 1, 2 * inner + 2, 2 * inner + 3]
    spots = []
    for mask in masks:
        owner = here ^ mask
        spots.append((owner // (2 * inner) != place) * inner + owner % inner)
    spots = jnp.stack(spots).astype(jnp.int32)

    gain = direct_gain.reshape(2, parts, devices // 2, 2 * pairs // parts)
    gain = lax.dynamic_index_in_dim(lax.dynamic_index_in_dim(gain, twin, 0, False), rank, 1, False)
    gain = jnp.broadcast_to(gain.reshape(2 * pairs, 1), (2 * pairs, LANES))

    half = channels // 2
    wide = depth
    padded = jnp.pad(edges[0], ((0, PACK - (TAPS - 1)), (0, 0)))
    asked = jnp.concatenate([query_feat, padded], axis=0)
    asked = lax.dynamic_slice_in_dim(asked, (1 - twin) * half, half, 1)
    asked = swap(asked, "seq", inner)
    asked_edge = asked[tokens : tokens + TAPS - 1]

    def at(i):
        return (i // (2 * inner) * inner + i % inner) * 2 + i // inner % 2

    groups = [[o * 2 * inner + t * inner + i for o in range(outer) for i in range(inner)] for t in range(2)]
    spreads, backs = [], []
    for part in range(parts):
        turned = mix(
            key_feat, value_feat, edges, short_filter, part, parts, outer, inner, long_filter
        )
        turned = turned.reshape(devices, 3 * pairs // parts, tokens)
        spreads.append(lax.all_to_all(turned, "seq", split_axis=0, concat_axis=0, tiled=True))
    for part in range(parts):
        chans = 2 * pairs // parts
        conv = convolve(spreads[part], spreads[part], chans, chans, gain, part, at)
        conv = conv.reshape(devices // 2, 2, 2 * pairs // parts, tokens)
        backs.append(
            lax.all_to_all(conv, "seq", split_axis=0, concat_axis=0, tiled=True, axis_index_groups=groups)
        )
    blocks = half // wide
    spot = jnp.stack([twin * blocks, twin * blocks, twin, 0 * twin, 1 - twin]).astype(jnp.int32)
    kept, given = [], []
    for part in range(parts):
        own, passed = gate(
            spot, short_filter, backs[part], part, wide, (query_feat, edges[0]), (asked, asked_edge)
        )
        kept.append(own)
        given.append(passed)
    kept_far, given_far = [], []
    for part in range(parts):
        given_far.append(swap(given[part], "ch", 1))
        kept_far.append(swap(kept[part], "ch", 1))
    sums, taken = [], []
    for cut in range(CUTS):
        passed = project(spots, given + given_far, pieces[cut], jnp.bfloat16, span, cut * span)
        taken.append(swap(passed, "seq", inner))
    for cut in range(CUTS):
        sums.append(project(spots, kept + kept_far, pieces[cut], jnp.float32, span, cut * span))
    outs = [(a + b.astype(jnp.float32)).astype(jnp.bfloat16) for a, b in zip(sums, taken)]
    return jnp.concatenate(outs, axis=1)


def solution(mesh):
    in_specs = (
        P("seq", "ch"),
        P("seq", "ch"),
        P("seq", "ch"),
        P(None, None, "ch"),
        P("ch", "seq"),
        P("ch"),
        P("seq", "ch"),
    )
    return jax.shard_map(layer, mesh=mesh, in_specs=in_specs, out_specs=P("seq", "ch"), check_vma=False)
```

```python
import functools

import jax
import jax.numpy as jnp
from jax import lax
from jax.experimental import pallas as pl
from jax.experimental.pallas import tpu as pltpu
from jax.sharding import PartitionSpec as P


TAPS = 3
PARTS = 2
CUTS = 2
LANES = 128
PACK = 16


def shifted(block, axis, distance):
    devices = range(lax.axis_size(axis))
    route = [(i - distance, i) for i in devices if i - distance in devices]
    return lax.ppermute(block, axis, route)


def featurized(inputs, edge, taps):
    rows = inputs.astype(jnp.float32)
    index = lax.broadcasted_iota(jnp.int32, rows.shape, 0)
    total = taps[0:1] * rows
    for tap in range(1, TAPS):
        moved = pltpu.roll(rows, tap, 0)
        for row in range(tap):
            first = TAPS - 1 - tap + row
            moved = jnp.where(index == row, edge[first : first + 1], moved)
        total = total + taps[tap : tap + 1] * moved
    return total


def mix_kernel(key_ref, value_ref, edge_ref, short_ref, *refs):
    sent_ref = refs[-1]
    outer, _, inner, _, tokens = sent_ref.shape
    edge = edge_ref[...].astype(jnp.float32)
    mixed = featurized(key_ref[...], edge[1], short_ref[1]) * featurized(
        value_ref[...], edge[2], short_ref[2]
    )
    each = mixed.shape[1] // (outer * inner)
    turned = mixed.T.astype(jnp.bfloat16)
    sent_ref[:, 0, :, 0:each, :] = turned.reshape(outer, inner, each, tokens)
    for taps_ref in refs[:-1]:
        taps = taps_ref[...].astype(jnp.bfloat16)
        sent_ref[:, 0, :, each:, :] = taps.reshape(outer, inner, each // 2, tokens)


def gate_kernel(count, *refs):
    short_ref = refs[0]
    for own in range(count):
        query_ref, edge_ref, conv_ref = refs[1 + 3 * own : 4 + 3 * own]
        gated_ref = refs[1 + 3 * count + own]
        edge = edge_ref[...].astype(jnp.float32)
        query_short = featurized(query_ref[...], edge, short_ref[0])
        wide, tokens = query_short.shape[1], query_short.shape[0]
        summed = conv_ref[...].astype(jnp.float32).reshape(wide, tokens).T
        gated_ref[0] = (query_short * summed).astype(jnp.bfloat16)


def conv_kernel(n, tok, width, place, x_ref, f_ref, gain_ref, y_ref, xi, xs, ys, fs):
    halves = tok // LANES
    groups = LANES // PACK
    for e in range(halves):
        for i in range(n):
            fs[:, i * halves + e, :] = f_ref[i, :, e * LANES : (e + 1) * LANES].astype(jnp.float32)
            xi[e, i * width : (i + 1) * width, :] = x_ref[
                i, :, e * LANES : (e + 1) * LANES
            ].astype(jnp.float32)
        for c in range(width):
            xs[e, c, 0:n, :] = jnp.zeros((n, LANES), jnp.float32)
            xs[e, c, n : 2 * n, :] = xi[e, pl.ds(c, n, stride=width), :]
    lane = lax.broadcasted_iota(jnp.int32, (PACK, LANES), 1)
    sub = lax.broadcasted_iota(jnp.int32, (PACK, LANES), 0)

    def one(p, carry):
        def skewed(m):
            if m == 0:
                return jnp.zeros((PACK, LANES), jnp.float32)
            row = fs[p, m - 1 : m, :]
            return pltpu.roll(
                jnp.broadcast_to(row, (PACK, LANES)), 0, 1, stride=1, stride_axis=0
            )

        def turns(m, part):
            now = skewed(m)
            base = jnp.where(lane >= sub, now, part).astype(jnp.bfloat16)
            return now, [base] + [
                pltpu.roll(base, LANES - PACK * k, 1) for k in range(1, groups)
            ]

        def stack(before, after):
            tiles = [after[0]]
            for k in range(groups - 1, 0, -1):
                tiles.append(jnp.where(lane < LANES - PACK * k, before[k], after[k]))
            return jnp.concatenate(tiles, axis=0)

        part, before = turns(0, skewed(0))
        old = jnp.zeros((LANES, LANES), jnp.bfloat16)
        acc = None
        for d in range(n):
            cols = [old]
            for e in range(halves):
                part, after = turns(d * halves + e + 1, part)
                cols.append(stack(before, after))
                before = after
            old = cols[-1]
            rhs = jnp.concatenate(
                [jnp.concatenate(cols[1:], axis=1), jnp.concatenate(cols[:-1], axis=1)], axis=0
            )
            lhs = jnp.concatenate(
                [
                    jnp.concatenate(
                        [
                            xs[e, 2 * p + c, n - d : 2 * n - d, :].astype(jnp.bfloat16)
                            for e in range(halves)
                        ],
                        axis=1,
                    )
                    for c in range(2)
                ],
                axis=0,
            )
            out = jnp.dot(lhs, rhs, preferred_element_type=jnp.float32)
            acc = out if acc is None else acc + out
        for e in range(halves):
            for c in range(2):
                ys[e, pl.ds(2 * p + c, n, stride=width), :] = acc[
                    c * n : (c + 1) * n, e * LANES : (e + 1) * LANES
                ]
        return carry

    lax.fori_loop(0, width // 2, one, 0, unroll=4 if n <= 16 else 1)
    for e in range(halves):
        for i in range(n):
            rows = slice(i * width, (i + 1) * width)
            total = ys[e, rows, :] + gain_ref[...] * xi[e, rows, :]
            y_ref[place(i), :, e * LANES : (e + 1) * LANES] = total.astype(jnp.bfloat16)


def convolve(x, f, skip, chans, gain, part, place):
    n, _, tok = x.shape
    width = min(16, chans)
    halves = tok // LANES
    assert halves == 2
    return pl.pallas_call(
        functools.partial(conv_kernel, n, tok, width, place),
        grid=(chans // width,),
        in_specs=[
            pl.BlockSpec((n, width, tok), lambda g: (0, g, 0)),
            pl.BlockSpec((n, width // 2, tok), lambda g: (0, g + skip // (width // 2), 0)),
            pl.BlockSpec((width, LANES), lambda g: (g + part * (chans // width), 0)),
        ],
        out_specs=pl.BlockSpec((n, width, tok), lambda g: (0, g, 0)),
        out_shape=jax.ShapeDtypeStruct((n, chans, tok), jnp.bfloat16),
        scratch_shapes=[
            pltpu.VMEM((halves, n * width, LANES), jnp.float32),
            pltpu.VMEM((halves, width, 2 * n, LANES), jnp.float32),
            pltpu.VMEM((halves, n * width, LANES), jnp.float32),
            pltpu.VMEM((width // 2, n * halves, LANES), jnp.float32),
        ],
        name="convolve",
    )(x, f, gain)


def mix(key_feat, value_feat, edges, short_filter, part, parts, outer, inner, *taps):
    tokens, channels = key_feat.shape
    wide = channels // (2 * parts)
    each = wide // (outer * inner)
    each += each // 2 * len(taps)
    rows = pl.BlockSpec((tokens, wide), lambda g: (0, g * parts + part))
    return pl.pallas_call(
        mix_kernel,
        grid=(2,),
        in_specs=[
            rows,
            rows,
            pl.BlockSpec((3, TAPS - 1, wide), lambda g: (0, 0, g * parts + part)),
            pl.BlockSpec((3, TAPS, wide), lambda g: (0, 0, g * parts + part)),
        ]
        + [pl.BlockSpec((wide // 2, tokens), lambda g: (g * parts + part, 0))] * len(taps),
        out_specs=pl.BlockSpec((outer, 1, inner, each, tokens), lambda g: (0, g, 0, 0, 0)),
        out_shape=jax.ShapeDtypeStruct((outer, 2, inner, each, tokens), jnp.bfloat16),
        name="mix",
    )(key_feat, value_feat, edges, short_filter, *taps)


def gate(spot, short_filter, conv, first, wide, *sources):
    count = len(sources)
    origins, _, each, tokens = conv.shape
    blocks = origins * each // wide
    per = wide // each
    specs, operands = [], []
    for own, (query, edge) in enumerate(sources):
        column = lambda g, spot, own=own: (0, spot[1 + 2 * own] + g + first * blocks)
        specs += [
            pl.BlockSpec((tokens, wide), column),
            pl.BlockSpec((TAPS - 1, wide), column),
            pl.BlockSpec((per, 1, each, tokens), lambda g, spot, own=own: (g, spot[2 + 2 * own], 0, 0)),
        ]
        operands += [query, edge, conv]
    return pl.pallas_call(
        lambda spot_ref, *refs: gate_kernel(count, *refs),
        grid_spec=pltpu.PrefetchScalarGridSpec(
            num_scalar_prefetch=1,
            grid=(blocks,),
            in_specs=[pl.BlockSpec((3, TAPS, wide), lambda g, spot: (0, 0, spot[0] + g + first * blocks))] + specs,
            out_specs=[pl.BlockSpec((1, tokens, wide), lambda g, spot: (g, 0, 0))] * count,
        ),
        out_shape=[jax.ShapeDtypeStruct((blocks, tokens, wide), jnp.bfloat16)] * count,
        name="gate",
    )(spot, short_filter, *operands)


def plain(query_feat, key_feat, value_feat, short_filter, long_filter, direct_gain, out_weight):
    tokens, channels = query_feat.shape
    devices = lax.axis_size("seq")
    pairs = long_filter.shape[0] // devices
    here = lax.axis_index("seq")
    weights = lax.all_gather(out_weight, "seq", axis=0, tiled=True)
    last = slice(tokens - (TAPS - 1), None)
    edges = shifted(jnp.stack([query_feat[last], key_feat[last], value_feat[last]]), "seq", 1)
    sent = long_filter.astype(jnp.bfloat16).reshape(devices, pairs, tokens)
    taps = lax.all_to_all(sent, "seq", split_axis=0, concat_axis=0, tiled=True)
    gain = lax.dynamic_index_in_dim(direct_gain.reshape(devices, 2 * pairs, 1), here, 0, False)
    gain = jnp.broadcast_to(gain, (2 * pairs, LANES))
    turned = mix(key_feat, value_feat, edges, short_filter, 0, 1, 1, devices // 2)
    turned = turned.reshape(devices, 2 * pairs, tokens)
    spread = lax.all_to_all(turned, "seq", split_axis=0, concat_axis=0, tiled=True)
    conv = convolve(spread, taps, 0, 2 * pairs, gain, 0, lambda i: i)
    conv = lax.all_to_all(conv, "seq", split_axis=0, concat_axis=0, tiled=True)
    wide = min(256, channels)
    spot = jnp.zeros((3,), jnp.int32)
    (gated,) = gate(spot, short_filter, conv[:, None], 0, wide, (query_feat, edges[0]))
    gated = gated.transpose(1, 0, 2).reshape(tokens, channels)
    features = lax.all_gather(gated, "ch", axis=1, tiled=True)
    return jnp.dot(features, weights, preferred_element_type=jnp.float32).astype(jnp.bfloat16)


def project_kernel(per, spots, *refs):
    gated, pieces = refs[: 2 * per], refs[2 * per : -3]
    more, pieces = pieces[: len(pieces) % 8], pieces[len(pieces) % 8 :]
    kept_ref, given_ref, rows = refs[-3:]
    blocks, tokens, wide = gated[0].shape
    count = len(pieces) // 2

    def run(first):
        @pl.when(pl.program_id(0) == 0)
        def _():
            for piece in range(count):
                spot = spots[first + piece]
                columns = slice(piece * wide, (piece + 1) * wide)
                for source in range(per):

                    @pl.when(spot // blocks == source)
                    def _():
                        rows[:tokens, columns] = gated[source][lax.rem(spot, blocks)]
                        rows[tokens:, columns] = gated[per + source][lax.rem(spot, blocks)]

        total = None
        for piece in range(count):
            out = jnp.dot(
                rows[:, piece * wide : (piece + 1) * wide],
                pieces[first + piece][...],
                preferred_element_type=jnp.float32,
            )
            total = out if total is None else total + out
        kept, given = total[:tokens], total[tokens:]
        if more:
            kept, given = kept + more[0][...], given + more[1][...]
        kept_ref[...] = kept
        given_ref[...] = given.astype(given_ref.dtype)

    @pl.when(spots[2 * count] == 0)
    def _():
        run(0)

    @pl.when(spots[2 * count] != 0)
    def _():
        run(count)


def project(spots, kept, given, pieces, columns, first, more=()):
    blocks, tokens, wide = kept[0].shape
    step = min(256, columns)

    def held(piece):
        skip = first // step if piece.shape[1] > columns else 0
        return pl.BlockSpec((wide, step), lambda j, spots: (0, j + skip))

    whole = pl.BlockSpec((blocks, tokens, wide), lambda j, spots: (0, 0, 0))
    out = pl.BlockSpec((tokens, step), lambda j, spots: (0, j))
    return pl.pallas_call(
        functools.partial(project_kernel, len(kept)),
        grid_spec=pltpu.PrefetchScalarGridSpec(
            num_scalar_prefetch=1,
            grid=(columns // step,),
            in_specs=[whole] * (2 * len(kept)) + [out] * len(more) + [held(piece) for piece in pieces],
            out_specs=[out, out],
            scratch_shapes=[pltpu.VMEM((2 * tokens, len(pieces) // 2 * wide), jnp.bfloat16)],
        ),
        out_shape=[
            jax.ShapeDtypeStruct((tokens, columns), jnp.float32),
            jax.ShapeDtypeStruct((tokens, columns), jnp.bfloat16 if more else jnp.float32),
        ],
        name="project",
    )(spots, *kept, *given, *more, *pieces)


def layer(query_feat, key_feat, value_feat, short_filter, long_filter, direct_gain, out_weight):
    tokens, channels = query_feat.shape
    devices = lax.axis_size("seq")
    sides = lax.axis_size("ch")
    here = lax.axis_index("seq")
    place = lax.axis_index("ch")
    depth, columns = out_weight.shape
    pairs = long_filter.shape[0] // devices
    inner, outer = 4, devices // 8
    small = sides == 2 and outer == 2 and depth % 256 == 0
    if not small:
        return plain(query_feat, key_feat, value_feat, short_filter, long_filter, direct_gain, out_weight)
    parts = PARTS
    twin = here // inner % 2
    rank = here // (2 * inner) * inner + here % inner

    def swap(block, axis, mask):
        return lax.ppermute(block, axis, [(i ^ mask, i) for i in range(lax.axis_size(axis))])

    last = slice(tokens - (TAPS - 1), None)
    edges = shifted(jnp.stack([query_feat[last], key_feat[last], value_feat[last]]), "seq", 1)

    near = swap(out_weight, "seq", 2)
    mate = swap(out_weight, "seq", 1)
    near_mate = swap(near, "seq", 1)
    span = columns // CUTS
    pieces = []
    for cut in range(CUTS):
        share = span // 2 if cut == 0 else span
        far = []
        for start in range(cut * span, (cut + 1) * span, share):
            far.append(swap(out_weight[:, start : start + share], "seq", 2 * inner))
        far = far[0] if len(far) == 1 else jnp.concatenate(far, axis=1)
        far_near = swap(far, "seq", 2)
        far_mate = swap(far, "seq", 1)
        far_near_mate = swap(far_near, "seq", 1)
        pieces.append(
            [out_weight, mate, near, near_mate, far, far_mate, far_near, far_near_mate]
        )
    masks = [0, 1, 2, 3, 2 * inner, 2 * inner + 1, 2 * inner + 2, 2 * inner + 3]
    spots = [(here ^ mask) % inner for mask in masks]
    apart = (here // (2 * inner) + place) % 2
    near_spots = jnp.stack(spots + [apart]).astype(jnp.int32)
    far_spots = jnp.stack(spots + [1 - apart]).astype(jnp.int32)

    gain = direct_gain.reshape(2, parts, devices // 2, 2 * pairs // parts)
    gain = lax.dynamic_index_in_dim(lax.dynamic_index_in_dim(gain, twin, 0, False), rank, 1, False)
    gain = jnp.broadcast_to(gain.reshape(2 * pairs, 1), (2 * pairs, LANES))

    half = channels // 2
    wide = depth
    padded = jnp.pad(edges[0], ((0, PACK - (TAPS - 1)), (0, 0)))
    asked = jnp.concatenate([query_feat, padded], axis=0)
    asked = lax.dynamic_slice_in_dim(asked, (1 - twin) * half, half, 1)
    asked = swap(asked, "seq", inner)
    asked_edge = asked[tokens : tokens + TAPS - 1]

    def at(i):
        return (i // (2 * inner) * inner + i % inner) * 2 + i // inner % 2

    groups = [[o * 2 * inner + t * inner + i for o in range(outer) for i in range(inner)] for t in range(2)]
    spreads, backs = [], []
    for part in range(parts):
        turned = mix(
            key_feat, value_feat, edges, short_filter, part, parts, outer, inner, long_filter
        )
        turned = turned.reshape(devices, 3 * pairs // parts, tokens)
        spreads.append(lax.all_to_all(turned, "seq", split_axis=0, concat_axis=0, tiled=True))
    for part in range(parts):
        chans = 2 * pairs // parts
        conv = convolve(spreads[part], spreads[part], chans, chans, gain, part, at)
        conv = conv.reshape(devices // 2, 2, 2 * pairs // parts, tokens)
        backs.append(
            lax.all_to_all(conv, "seq", split_axis=0, concat_axis=0, tiled=True, axis_index_groups=groups)
        )
    blocks = half // wide
    spot = jnp.stack([twin * blocks, twin * blocks, twin, 0 * twin, 1 - twin]).astype(jnp.int32)
    kept, given = [], []
    for part in range(parts):
        own, passed = gate(
            spot, short_filter, backs[part], part, wide, (query_feat, edges[0]), (asked, asked_edge)
        )
        kept.append(own)
        given.append(passed)
    kept_far, given_far = [], []
    for part in range(parts):
        given_far.append(swap(given[part], "ch", 1))
        kept_far.append(swap(kept[part], "ch", 1))
    sums, taken = [], []
    halves = []
    for cut in range(CUTS):
        halves.append(project(near_spots, kept, given, pieces[cut], span, cut * span))
    for cut in range(CUTS):
        held, passed = project(
            far_spots, kept_far, given_far, pieces[cut], span, cut * span, halves[cut]
        )
        sums.append(held)
        taken.append(swap(passed, "seq", inner))
    outs = [(a + b.astype(jnp.float32)).astype(jnp.bfloat16) for a, b in zip(sums, taken)]
    return jnp.concatenate(outs, axis=1)


def solution(mesh):
    in_specs = (
        P("seq", "ch"),
        P("seq", "ch"),
        P("seq", "ch"),
        P(None, None, "ch"),
        P("ch", "seq"),
        P("ch"),
        P("seq", "ch"),
    )
    return jax.shard_map(layer, mesh=mesh, in_specs=in_specs, out_specs=P("seq", "ch"), check_vma=False)
```

```python
import functools

import jax
import jax.numpy as jnp
from jax import lax
from jax.experimental import pallas as pl
from jax.experimental.pallas import tpu as pltpu
from jax.sharding import PartitionSpec as P


TAPS = 3
PARTS = 2
CUTS = 2
LANES = 128
PACK = 16


def shifted(block, axis, distance):
    devices = range(lax.axis_size(axis))
    route = [(i - distance, i) for i in devices if i - distance in devices]
    return lax.ppermute(block, axis, route)


def featurized(inputs, edge, taps):
    rows = inputs.astype(jnp.float32)
    index = lax.broadcasted_iota(jnp.int32, rows.shape, 0)
    total = taps[0:1] * rows
    for tap in range(1, TAPS):
        moved = pltpu.roll(rows, tap, 0)
        for row in range(tap):
            first = TAPS - 1 - tap + row
            moved = jnp.where(index == row, edge[first : first + 1], moved)
        total = total + taps[tap : tap + 1] * moved
    return total


def mix_kernel(key_ref, value_ref, edge_ref, short_ref, *refs):
    sent_ref = refs[-1]
    outer, _, inner, _, tokens = sent_ref.shape
    edge = edge_ref[...].astype(jnp.float32)
    mixed = featurized(key_ref[...], edge[1], short_ref[1]) * featurized(
        value_ref[...], edge[2], short_ref[2]
    )
    each = mixed.shape[1] // (outer * inner)
    turned = mixed.T.astype(jnp.bfloat16)
    sent_ref[:, 0, :, 0:each, :] = turned.reshape(outer, inner, each, tokens)
    for taps_ref in refs[:-1]:
        taps = taps_ref[...].astype(jnp.bfloat16)
        sent_ref[:, 0, :, each:, :] = taps.reshape(outer, inner, each // 2, tokens)


def gate_kernel(count, *refs):
    short_ref = refs[0]
    for own in range(count):
        query_ref, edge_ref, conv_ref = refs[1 + 3 * own : 4 + 3 * own]
        gated_ref = refs[1 + 3 * count + own]
        edge = edge_ref[...].astype(jnp.float32)
        query_short = featurized(query_ref[...], edge, short_ref[0])
        wide, tokens = query_short.shape[1], query_short.shape[0]
        summed = conv_ref[...].astype(jnp.float32).reshape(wide, tokens).T
        gated_ref[0] = (query_short * summed).astype(jnp.bfloat16)


def conv_kernel(n, tok, width, place, x_ref, f_ref, gain_ref, y_ref, xi, xs, ys, fs):
    halves = tok // LANES
    groups = LANES // PACK
    for e in range(halves):
        for i in range(n):
            fs[:, i * halves + e, :] = f_ref[i, :, e * LANES : (e + 1) * LANES].astype(jnp.float32)
            xi[e, i * width : (i + 1) * width, :] = x_ref[
                i, :, e * LANES : (e + 1) * LANES
            ].astype(jnp.float32)
        for c in range(width):
            xs[e, c, 0:n, :] = jnp.zeros((n, LANES), jnp.float32)
            xs[e, c, n : 2 * n, :] = xi[e, pl.ds(c, n, stride=width), :]
    lane = lax.broadcasted_iota(jnp.int32, (PACK, LANES), 1)
    sub = lax.broadcasted_iota(jnp.int32, (PACK, LANES), 0)

    def one(p, carry):
        def skewed(m):
            if m == 0:
                return jnp.zeros((PACK, LANES), jnp.float32)
            row = fs[p, m - 1 : m, :]
            return pltpu.roll(
                jnp.broadcast_to(row, (PACK, LANES)), 0, 1, stride=1, stride_axis=0
            )

        def turns(m, part):
            now = skewed(m)
            base = jnp.where(lane >= sub, now, part).astype(jnp.bfloat16)
            return now, [base] + [
                pltpu.roll(base, LANES - PACK * k, 1) for k in range(1, groups)
            ]

        def stack(before, after):
            tiles = [after[0]]
            for k in range(groups - 1, 0, -1):
                tiles.append(jnp.where(lane < LANES - PACK * k, before[k], after[k]))
            return jnp.concatenate(tiles, axis=0)

        part, before = turns(0, skewed(0))
        old = jnp.zeros((LANES, LANES), jnp.bfloat16)
        acc = None
        for d in range(n):
            cols = [old]
            for e in range(halves):
                part, after = turns(d * halves + e + 1, part)
                cols.append(stack(before, after))
                before = after
            old = cols[-1]
            rhs = jnp.concatenate(
                [jnp.concatenate(cols[1:], axis=1), jnp.concatenate(cols[:-1], axis=1)], axis=0
            )
            lhs = jnp.concatenate(
                [
                    jnp.concatenate(
                        [
                            xs[e, 2 * p + c, n - d : 2 * n - d, :].astype(jnp.bfloat16)
                            for e in range(halves)
                        ],
                        axis=1,
                    )
                    for c in range(2)
                ],
                axis=0,
            )
            out = jnp.dot(lhs, rhs, preferred_element_type=jnp.float32)
            acc = out if acc is None else acc + out
        for e in range(halves):
            for c in range(2):
                ys[e, pl.ds(2 * p + c, n, stride=width), :] = acc[
                    c * n : (c + 1) * n, e * LANES : (e + 1) * LANES
                ]
        return carry

    lax.fori_loop(0, width // 2, one, 0, unroll=4 if n <= 16 else 1)
    for e in range(halves):
        for i in range(n):
            rows = slice(i * width, (i + 1) * width)
            total = ys[e, rows, :] + gain_ref[...] * xi[e, rows, :]
            y_ref[place(i), :, e * LANES : (e + 1) * LANES] = total.astype(jnp.bfloat16)


def convolve(x, f, skip, chans, gain, part, place):
    n, _, tok = x.shape
    width = min(16, chans)
    halves = tok // LANES
    assert halves == 2
    return pl.pallas_call(
        functools.partial(conv_kernel, n, tok, width, place),
        grid=(chans // width,),
        in_specs=[
            pl.BlockSpec((n, width, tok), lambda g: (0, g, 0)),
            pl.BlockSpec((n, width // 2, tok), lambda g: (0, g + skip // (width // 2), 0)),
            pl.BlockSpec((width, LANES), lambda g: (g + part * (chans // width), 0)),
        ],
        out_specs=pl.BlockSpec((n, width, tok), lambda g: (0, g, 0)),
        out_shape=jax.ShapeDtypeStruct((n, chans, tok), jnp.bfloat16),
        scratch_shapes=[
            pltpu.VMEM((halves, n * width, LANES), jnp.float32),
            pltpu.VMEM((halves, width, 2 * n, LANES), jnp.float32),
            pltpu.VMEM((halves, n * width, LANES), jnp.float32),
            pltpu.VMEM((width // 2, n * halves, LANES), jnp.float32),
        ],
        name="convolve",
    )(x, f, gain)


def mix(key_feat, value_feat, edges, short_filter, part, parts, outer, inner, *taps):
    tokens, channels = key_feat.shape
    wide = channels // (2 * parts)
    each = wide // (outer * inner)
    each += each // 2 * len(taps)
    rows = pl.BlockSpec((tokens, wide), lambda g: (0, g * parts + part))
    return pl.pallas_call(
        mix_kernel,
        grid=(2,),
        in_specs=[
            rows,
            rows,
            pl.BlockSpec((3, TAPS - 1, wide), lambda g: (0, 0, g * parts + part)),
            pl.BlockSpec((3, TAPS, wide), lambda g: (0, 0, g * parts + part)),
        ]
        + [pl.BlockSpec((wide // 2, tokens), lambda g: (g * parts + part, 0))] * len(taps),
        out_specs=pl.BlockSpec((outer, 1, inner, each, tokens), lambda g: (0, g, 0, 0, 0)),
        out_shape=jax.ShapeDtypeStruct((outer, 2, inner, each, tokens), jnp.bfloat16),
        name="mix",
    )(key_feat, value_feat, edges, short_filter, *taps)


def gate(spot, short_filter, conv, first, wide, *sources):
    count = len(sources)
    origins, _, each, tokens = conv.shape
    blocks = origins * each // wide
    per = wide // each
    specs, operands = [], []
    for own, (query, edge) in enumerate(sources):
        column = lambda g, spot, own=own: (0, spot[1 + 2 * own] + g + first * blocks)
        specs += [
            pl.BlockSpec((tokens, wide), column),
            pl.BlockSpec((TAPS - 1, wide), column),
            pl.BlockSpec((per, 1, each, tokens), lambda g, spot, own=own: (g, spot[2 + 2 * own], 0, 0)),
        ]
        operands += [query, edge, conv]
    return pl.pallas_call(
        lambda spot_ref, *refs: gate_kernel(count, *refs),
        grid_spec=pltpu.PrefetchScalarGridSpec(
            num_scalar_prefetch=1,
            grid=(blocks,),
            in_specs=[pl.BlockSpec((3, TAPS, wide), lambda g, spot: (0, 0, spot[0] + g + first * blocks))] + specs,
            out_specs=[pl.BlockSpec((1, tokens, wide), lambda g, spot: (g, 0, 0))] * count,
        ),
        out_shape=[jax.ShapeDtypeStruct((blocks, tokens, wide), jnp.bfloat16)] * count,
        name="gate",
    )(spot, short_filter, *operands)


def plain(query_feat, key_feat, value_feat, short_filter, long_filter, direct_gain, out_weight):
    tokens, channels = query_feat.shape
    devices = lax.axis_size("seq")
    pairs = long_filter.shape[0] // devices
    here = lax.axis_index("seq")
    weights = lax.all_gather(out_weight, "seq", axis=0, tiled=True)
    last = slice(tokens - (TAPS - 1), None)
    edges = shifted(jnp.stack([query_feat[last], key_feat[last], value_feat[last]]), "seq", 1)
    sent = long_filter.astype(jnp.bfloat16).reshape(devices, pairs, tokens)
    taps = lax.all_to_all(sent, "seq", split_axis=0, concat_axis=0, tiled=True)
    gain = lax.dynamic_index_in_dim(direct_gain.reshape(devices, 2 * pairs, 1), here, 0, False)
    gain = jnp.broadcast_to(gain, (2 * pairs, LANES))
    turned = mix(key_feat, value_feat, edges, short_filter, 0, 1, 1, devices // 2)
    turned = turned.reshape(devices, 2 * pairs, tokens)
    spread = lax.all_to_all(turned, "seq", split_axis=0, concat_axis=0, tiled=True)
    conv = convolve(spread, taps, 0, 2 * pairs, gain, 0, lambda i: i)
    conv = lax.all_to_all(conv, "seq", split_axis=0, concat_axis=0, tiled=True)
    wide = min(256, channels)
    spot = jnp.zeros((3,), jnp.int32)
    (gated,) = gate(spot, short_filter, conv[:, None], 0, wide, (query_feat, edges[0]))
    gated = gated.transpose(1, 0, 2).reshape(tokens, channels)
    features = lax.all_gather(gated, "ch", axis=1, tiled=True)
    return jnp.dot(features, weights, preferred_element_type=jnp.float32).astype(jnp.bfloat16)


def project_kernel(count, per, spots, *refs):
    gated, pieces = refs[: 2 * per], refs[2 * per : 2 * per + count]
    kept_ref, given_ref, rows = refs[2 * per + count :]
    blocks, tokens, wide = gated[0].shape

    @pl.when(pl.program_id(0) == 0)
    def _():
        for piece in range(count):
            spot = spots[piece]
            columns = slice(piece * wide, (piece + 1) * wide)
            for source in range(per):

                @pl.when(spot // blocks == source)
                def _():
                    rows[:tokens, columns] = gated[source][lax.rem(spot, blocks)]
                    rows[tokens:, columns] = gated[per + source][lax.rem(spot, blocks)]

    total = None
    for piece in range(count):
        out = jnp.dot(
            rows[:, piece * wide : (piece + 1) * wide],
            pieces[piece][...],
            preferred_element_type=jnp.float32,
        )
        total = out if total is None else total + out
    kept_ref[...] = total[:tokens]
    given_ref[...] = total[tokens:].astype(jnp.bfloat16)


def project(spots, kept, given, pieces, columns, first):
    blocks, tokens, wide = kept[0].shape
    count = len(pieces)
    step = min(512, columns)

    def held(piece):
        skip = first // step if piece.shape[1] > columns else 0
        return pl.BlockSpec((wide, step), lambda j, spots: (0, j + skip))

    whole = pl.BlockSpec((blocks, tokens, wide), lambda j, spots: (0, 0, 0))
    out = pl.BlockSpec((tokens, step), lambda j, spots: (0, j))
    return pl.pallas_call(
        functools.partial(project_kernel, count, len(kept)),
        grid_spec=pltpu.PrefetchScalarGridSpec(
            num_scalar_prefetch=1,
            grid=(columns // step,),
            in_specs=[whole] * (2 * len(kept)) + [held(piece) for piece in pieces],
            out_specs=[out, out],
            scratch_shapes=[pltpu.VMEM((2 * tokens, count * wide), jnp.bfloat16)],
        ),
        out_shape=[
            jax.ShapeDtypeStruct((tokens, columns), jnp.float32),
            jax.ShapeDtypeStruct((tokens, columns), jnp.bfloat16),
        ],
        name="project",
    )(spots, *kept, *given, *pieces)


def layer(query_feat, key_feat, value_feat, short_filter, long_filter, direct_gain, out_weight):
    tokens, channels = query_feat.shape
    devices = lax.axis_size("seq")
    sides = lax.axis_size("ch")
    here = lax.axis_index("seq")
    place = lax.axis_index("ch")
    depth, columns = out_weight.shape
    pairs = long_filter.shape[0] // devices
    inner, outer = 4, devices // 8
    small = sides == 2 and outer == 2 and depth % 256 == 0
    if not small:
        return plain(query_feat, key_feat, value_feat, short_filter, long_filter, direct_gain, out_weight)
    parts = PARTS
    twin = here // inner % 2
    rank = here // (2 * inner) * inner + here % inner

    def swap(block, axis, mask):
        return lax.ppermute(block, axis, [(i ^ mask, i) for i in range(lax.axis_size(axis))])

    last = slice(tokens - (TAPS - 1), None)
    edges = shifted(jnp.stack([query_feat[last], key_feat[last], value_feat[last]]), "seq", 1)

    near = swap(out_weight, "seq", 2)
    mate = swap(out_weight, "seq", 1)
    near_mate = swap(near, "seq", 1)
    span = columns // CUTS
    pieces = []
    for cut in range(CUTS):
        share = span // 2 if cut == 0 else span
        far = []
        for start in range(cut * span, (cut + 1) * span, share):
            far.append(swap(out_weight[:, start : start + share], "seq", 2 * inner))
        far = far[0] if len(far) == 1 else jnp.concatenate(far, axis=1)
        far_near = swap(far, "seq", 2)
        far_mate = swap(far, "seq", 1)
        far_near_mate = swap(far_near, "seq", 1)
        pieces.append(
            [out_weight, mate, near, near_mate, far, far_mate, far_near, far_near_mate]
        )
    masks = [0, 1, 2, 3, 2 * inner, 2 * inner + 1, 2 * inner + 2, 2 * inner + 3]
    spots = []
    for mask in masks:
        owner = here ^ mask
        spots.append((owner // (2 * inner) != place) * inner + owner % inner)
    spots = jnp.stack(spots).astype(jnp.int32)

    gain = direct_gain.reshape(2, parts, devices // 2, 2 * pairs // parts)
    gain = lax.dynamic_index_in_dim(lax.dynamic_index_in_dim(gain, twin, 0, False), rank, 1, False)
    gain = jnp.broadcast_to(gain.reshape(2 * pairs, 1), (2 * pairs, LANES))

    half = channels // 2
    wide = depth
    padded = jnp.pad(edges[0], ((0, PACK - (TAPS - 1)), (0, 0)))
    asked = jnp.concatenate([query_feat, padded], axis=0)
    asked = lax.dynamic_slice_in_dim(asked, (1 - twin) * half, half, 1)
    asked = swap(asked, "seq", inner)
    asked_edge = asked[tokens : tokens + TAPS - 1]

    def at(i):
        return (i // (2 * inner) * inner + i % inner) * 2 + i // inner % 2

    groups = [[o * 2 * inner + t * inner + i for o in range(outer) for i in range(inner)] for t in range(2)]
    spreads, backs = [], []
    for part in range(parts):
        turned = mix(
            key_feat, value_feat, edges, short_filter, part, parts, outer, inner, long_filter
        )
        turned = turned.reshape(devices, 3 * pairs // parts, tokens)
        spreads.append(lax.all_to_all(turned, "seq", split_axis=0, concat_axis=0, tiled=True))
    for part in range(parts):
        chans = 2 * pairs // parts
        conv = convolve(spreads[part], spreads[part], chans, chans, gain, part, at)
        conv = conv.reshape(devices // 2, 2, 2 * pairs // parts, tokens)
        backs.append(
            lax.all_to_all(conv, "seq", split_axis=0, concat_axis=0, tiled=True, axis_index_groups=groups)
        )
    blocks = half // wide
    spot = jnp.stack([twin * blocks, twin * blocks, twin, 0 * twin, 1 - twin]).astype(jnp.int32)
    kept, given = [], []
    for part in range(parts):
        own, passed = gate(
            spot, short_filter, backs[part], part, wide, (query_feat, edges[0]), (asked, asked_edge)
        )
        kept.append(own)
        given.append(passed)
    kept_far, given_far = [], []
    for part in range(parts):
        given_far.append(swap(given[part], "ch", 1))
        kept_far.append(swap(kept[part], "ch", 1))
    sums, taken = [], []
    for cut in range(CUTS):
        held, passed = project(
            spots, kept + kept_far, given + given_far, pieces[cut], span, cut * span
        )
        sums.append(held)
        taken.append(swap(passed, "seq", inner))
    outs = [(a + b.astype(jnp.float32)).astype(jnp.bfloat16) for a, b in zip(sums, taken)]
    return jnp.concatenate(outs, axis=1)


def solution(mesh):
    in_specs = (
        P("seq", "ch"),
        P("seq", "ch"),
        P("seq", "ch"),
        P(None, None, "ch"),
        P("ch", "seq"),
        P("ch"),
        P("seq", "ch"),
    )
    return jax.shard_map(layer, mesh=mesh, in_specs=in_specs, out_specs=P("seq", "ch"), check_vma=False)
```

```python
import functools

import jax
import jax.numpy as jnp
from jax import lax
from jax.experimental import pallas as pl
from jax.experimental.pallas import tpu as pltpu
from jax.sharding import PartitionSpec as P


TAPS = 3
PARTS = (1, 1)
CUTS = 2
LANES = 128
PACK = 16


def shifted(block, axis, distance):
    devices = range(lax.axis_size(axis))
    route = [(i - distance, i) for i in devices if i - distance in devices]
    return lax.ppermute(block, axis, route)


def featurized(inputs, edge, taps):
    rows = inputs.astype(jnp.float32)
    index = lax.broadcasted_iota(jnp.int32, rows.shape, 0)
    total = taps[0:1] * rows
    for tap in range(1, TAPS):
        moved = pltpu.roll(rows, tap, 0)
        for row in range(tap):
            first = TAPS - 1 - tap + row
            moved = jnp.where(index == row, edge[first : first + 1], moved)
        total = total + taps[tap : tap + 1] * moved
    return total


def mix_kernel(key_ref, value_ref, edge_ref, short_ref, *refs):
    sent_ref = refs[-1]
    outer, _, inner, _, tokens = sent_ref.shape
    edge = edge_ref[...].astype(jnp.float32)
    mixed = featurized(key_ref[...], edge[1], short_ref[1]) * featurized(
        value_ref[...], edge[2], short_ref[2]
    )
    each = mixed.shape[1] // (outer * inner)
    turned = mixed.T.astype(jnp.bfloat16)
    sent_ref[:, 0, :, 0:each, :] = turned.reshape(outer, inner, each, tokens)
    for taps_ref in refs[:-1]:
        taps = taps_ref[...].astype(jnp.bfloat16)
        sent_ref[:, 0, :, each:, :] = taps.reshape(outer, inner, each // 2, tokens)


def gate_kernel(count, *refs):
    short_ref = refs[0]
    for own in range(count):
        query_ref, edge_ref, conv_ref = refs[1 + 3 * own : 4 + 3 * own]
        gated_ref = refs[1 + 3 * count + own]
        edge = edge_ref[...].astype(jnp.float32)
        query_short = featurized(query_ref[...], edge, short_ref[0])
        wide, tokens = query_short.shape[1], query_short.shape[0]
        summed = conv_ref[...].astype(jnp.float32).reshape(wide, tokens).T
        gated_ref[0] = (query_short * summed).astype(jnp.bfloat16)


def conv_kernel(n, tok, width, place, x_ref, f_ref, gain_ref, y_ref, xi, xs, ys, fs):
    halves = tok // LANES
    groups = LANES // PACK
    for e in range(halves):
        for i in range(n):
            fs[:, i * halves + e, :] = f_ref[i, :, e * LANES : (e + 1) * LANES].astype(jnp.float32)
            xi[e, i * width : (i + 1) * width, :] = x_ref[
                i, :, e * LANES : (e + 1) * LANES
            ].astype(jnp.float32)
        for c in range(width):
            xs[e, c, 0:n, :] = jnp.zeros((n, LANES), jnp.float32)
            xs[e, c, n : 2 * n, :] = xi[e, pl.ds(c, n, stride=width), :]
    lane = lax.broadcasted_iota(jnp.int32, (PACK, LANES), 1)
    sub = lax.broadcasted_iota(jnp.int32, (PACK, LANES), 0)

    def one(p, carry):
        def skewed(m):
            if m == 0:
                return jnp.zeros((PACK, LANES), jnp.float32)
            row = fs[p, m - 1 : m, :]
            return pltpu.roll(
                jnp.broadcast_to(row, (PACK, LANES)), 0, 1, stride=1, stride_axis=0
            )

        def turns(m, part):
            now = skewed(m)
            base = jnp.where(lane >= sub, now, part).astype(jnp.bfloat16)
            return now, [base] + [
                pltpu.roll(base, LANES - PACK * k, 1) for k in range(1, groups)
            ]

        def stack(before, after):
            tiles = [after[0]]
            for k in range(groups - 1, 0, -1):
                tiles.append(jnp.where(lane < LANES - PACK * k, before[k], after[k]))
            return jnp.concatenate(tiles, axis=0)

        part, before = turns(0, skewed(0))
        old = jnp.zeros((LANES, LANES), jnp.bfloat16)
        acc = None
        for d in range(n):
            cols = [old]
            for e in range(halves):
                part, after = turns(d * halves + e + 1, part)
                cols.append(stack(before, after))
                before = after
            old = cols[-1]
            rhs = jnp.concatenate(
                [jnp.concatenate(cols[1:], axis=1), jnp.concatenate(cols[:-1], axis=1)], axis=0
            )
            lhs = jnp.concatenate(
                [
                    jnp.concatenate(
                        [
                            xs[e, 2 * p + c, n - d : 2 * n - d, :].astype(jnp.bfloat16)
                            for e in range(halves)
                        ],
                        axis=1,
                    )
                    for c in range(2)
                ],
                axis=0,
            )
            out = jnp.dot(lhs, rhs, preferred_element_type=jnp.float32)
            acc = out if acc is None else acc + out
        for e in range(halves):
            for c in range(2):
                ys[e, pl.ds(2 * p + c, n, stride=width), :] = acc[
                    c * n : (c + 1) * n, e * LANES : (e + 1) * LANES
                ]
        return carry

    lax.fori_loop(0, width // 2, one, 0, unroll=4 if n <= 16 else 1)
    for e in range(halves):
        for i in range(n):
            rows = slice(i * width, (i + 1) * width)
            total = ys[e, rows, :] + gain_ref[...] * xi[e, rows, :]
            y_ref[place(i), :, e * LANES : (e + 1) * LANES] = total.astype(jnp.bfloat16)


def convolve(x, f, chans, gain, place, x_at, f_at, gain_at):
    n, _, tok = x.shape
    width = min(16, chans)
    halves = tok // LANES
    assert halves == 2
    return pl.pallas_call(
        functools.partial(conv_kernel, n, tok, width, place),
        grid=(chans // width,),
        in_specs=[
            pl.BlockSpec((n, width, tok), lambda g: (0, x_at(g), 0)),
            pl.BlockSpec((n, width // 2, tok), lambda g: (0, f_at(g), 0)),
            pl.BlockSpec((width, LANES), lambda g: (gain_at(g), 0)),
        ],
        out_specs=pl.BlockSpec((n, width, tok), lambda g: (0, g, 0)),
        out_shape=jax.ShapeDtypeStruct((n, chans, tok), jnp.bfloat16),
        scratch_shapes=[
            pltpu.VMEM((halves, n * width, LANES), jnp.float32),
            pltpu.VMEM((halves, width, 2 * n, LANES), jnp.float32),
            pltpu.VMEM((halves, n * width, LANES), jnp.float32),
            pltpu.VMEM((width // 2, n * halves, LANES), jnp.float32),
        ],
        name="convolve",
    )(x, f, gain)


def mix(key_feat, value_feat, edges, short_filter, start, blocks, wide, outer, inner, *taps):
    tokens, channels = key_feat.shape
    each = wide // (outer * inner)
    each += each // 2 * len(taps)
    per = channels // (2 * wide)
    rows = pl.BlockSpec((tokens, wide), lambda t, g: (0, t * per + start + g))
    return pl.pallas_call(
        mix_kernel,
        grid=(2, blocks),
        in_specs=[
            rows,
            rows,
            pl.BlockSpec((3, TAPS - 1, wide), lambda t, g: (0, 0, t * per + start + g)),
            pl.BlockSpec((3, TAPS, wide), lambda t, g: (0, 0, t * per + start + g)),
        ]
        + [pl.BlockSpec((wide // 2, tokens), lambda t, g: (t * per + start + g, 0))] * len(taps),
        out_specs=pl.BlockSpec((outer, 1, inner, each, tokens), lambda t, g: (0, t, 0, g, 0)),
        out_shape=jax.ShapeDtypeStruct((outer, 2, inner, blocks * each, tokens), jnp.bfloat16),
        name="mix",
    )(key_feat, value_feat, edges, short_filter, *taps)


def gate(spot, short_filter, conv, first, wide, *sources):
    count = len(sources)
    origins, _, chans, tokens = conv.shape
    blocks = origins * chans // wide
    each = max(wide // origins, 1)
    each = each if chans % each == 0 and each % 8 == 0 else chans
    per = wide // each
    specs, operands = [], []
    for own, (query, edge) in enumerate(sources):
        column = lambda g, spot, own=own: (0, spot[1 + 2 * own] + g + first)

        def part(g, spot, own=own):
            return (0, spot[2 + 2 * own], g, 0) if per == origins else (g, spot[2 + 2 * own], 0, 0)

        specs += [
            pl.BlockSpec((tokens, wide), column),
            pl.BlockSpec((TAPS - 1, wide), column),
            pl.BlockSpec((per, 1, each, tokens), part),
        ]
        operands += [query, edge, conv]
    return pl.pallas_call(
        lambda spot_ref, *refs: gate_kernel(count, *refs),
        grid_spec=pltpu.PrefetchScalarGridSpec(
            num_scalar_prefetch=1,
            grid=(blocks,),
            in_specs=[pl.BlockSpec((3, TAPS, wide), lambda g, spot: (0, 0, spot[0] + g + first))] + specs,
            out_specs=[pl.BlockSpec((1, tokens, wide), lambda g, spot: (g, 0, 0))] * count,
        ),
        out_shape=[jax.ShapeDtypeStruct((blocks, tokens, wide), jnp.bfloat16)] * count,
        name="gate",
    )(spot, short_filter, *operands)


def plain(query_feat, key_feat, value_feat, short_filter, long_filter, direct_gain, out_weight):
    tokens, channels = query_feat.shape
    devices = lax.axis_size("seq")
    pairs = long_filter.shape[0] // devices
    here = lax.axis_index("seq")
    weights = lax.all_gather(out_weight, "seq", axis=0, tiled=True)
    last = slice(tokens - (TAPS - 1), None)
    edges = shifted(jnp.stack([query_feat[last], key_feat[last], value_feat[last]]), "seq", 1)
    sent = long_filter.astype(jnp.bfloat16).reshape(devices, pairs, tokens)
    taps = lax.all_to_all(sent, "seq", split_axis=0, concat_axis=0, tiled=True)
    gain = lax.dynamic_index_in_dim(direct_gain.reshape(devices, 2 * pairs, 1), here, 0, False)
    gain = jnp.broadcast_to(gain, (2 * pairs, LANES))
    turned = mix(key_feat, value_feat, edges, short_filter, 0, 1, channels // 2, 1, devices // 2)
    turned = turned.reshape(devices, 2 * pairs, tokens)
    spread = lax.all_to_all(turned, "seq", split_axis=0, concat_axis=0, tiled=True)
    same = lambda i: i
    conv = convolve(spread, taps, 2 * pairs, gain, same, same, same, same)
    conv = lax.all_to_all(conv, "seq", split_axis=0, concat_axis=0, tiled=True)
    wide = min(256, channels)
    spot = jnp.zeros((3,), jnp.int32)
    (gated,) = gate(spot, short_filter, conv[:, None], 0, wide, (query_feat, edges[0]))
    gated = gated.transpose(1, 0, 2).reshape(tokens, channels)
    features = lax.all_gather(gated, "ch", axis=1, tiled=True)
    return jnp.dot(features, weights, preferred_element_type=jnp.float32).astype(jnp.bfloat16)


def project_kernel(count, per, spots, *refs):
    gated, pieces = refs[: 2 * per], refs[2 * per : 2 * per + count]
    kept_ref, given_ref, rows = refs[2 * per + count :]
    tokens, wide = gated[0].shape[1:]
    places = [(source, block) for source in range(per) for block in range(gated[source].shape[0])]

    @pl.when(pl.program_id(0) == 0)
    def _():
        for piece in range(count):
            spot = spots[piece]
            columns = slice(piece * wide, (piece + 1) * wide)
            for value, (source, block) in enumerate(places):

                @pl.when(spot == value)
                def _():
                    rows[:tokens, columns] = gated[source][block]
                    rows[tokens:, columns] = gated[per + source][block]

    total = None
    for piece in range(count):
        out = jnp.dot(
            rows[:, piece * wide : (piece + 1) * wide],
            pieces[piece][...],
            preferred_element_type=jnp.float32,
        )
        total = out if total is None else total + out
    kept_ref[...] = total[:tokens]
    given_ref[...] = total[tokens:].astype(jnp.bfloat16)


def project(spots, kept, given, pieces, columns, first):
    tokens, wide = kept[0].shape[1:]
    count = len(pieces)
    step = min(512, columns)

    def held(piece):
        skip = first // step if piece.shape[1] > columns else 0
        return pl.BlockSpec((wide, step), lambda j, spots: (0, j + skip))

    whole = [pl.BlockSpec(block.shape, lambda j, spots: (0, 0, 0)) for block in (*kept, *given)]
    out = pl.BlockSpec((tokens, step), lambda j, spots: (0, j))
    return pl.pallas_call(
        functools.partial(project_kernel, count, len(kept)),
        grid_spec=pltpu.PrefetchScalarGridSpec(
            num_scalar_prefetch=1,
            grid=(columns // step,),
            in_specs=whole + [held(piece) for piece in pieces],
            out_specs=[out, out],
            scratch_shapes=[pltpu.VMEM((2 * tokens, count * wide), jnp.bfloat16)],
        ),
        out_shape=[
            jax.ShapeDtypeStruct((tokens, columns), jnp.float32),
            jax.ShapeDtypeStruct((tokens, columns), jnp.bfloat16),
        ],
        name="project",
    )(spots, *kept, *given, *pieces)


def layer(query_feat, key_feat, value_feat, short_filter, long_filter, direct_gain, out_weight):
    tokens, channels = query_feat.shape
    devices = lax.axis_size("seq")
    sides = lax.axis_size("ch")
    here = lax.axis_index("seq")
    place = lax.axis_index("ch")
    depth, columns = out_weight.shape
    pairs = long_filter.shape[0] // devices
    inner, outer = 4, devices // 8
    small = sides == 2 and outer == 2 and depth % 256 == 0
    if not small:
        return plain(query_feat, key_feat, value_feat, short_filter, long_filter, direct_gain, out_weight)
    half = channels // 2
    wide = depth
    parts = [half // wide * share // sum(PARTS) for share in PARTS]
    starts = [sum(parts[:part]) for part in range(len(parts))]
    each = wide // (devices // 2)
    twin = here // inner % 2
    rank = here // (2 * inner) * inner + here % inner

    def swap(block, axis, mask):
        return lax.ppermute(block, axis, [(i ^ mask, i) for i in range(lax.axis_size(axis))])

    last = slice(tokens - (TAPS - 1), None)
    edges = shifted(jnp.stack([query_feat[last], key_feat[last], value_feat[last]]), "seq", 1)

    near = swap(out_weight, "seq", 2)
    mate = swap(out_weight, "seq", 1)
    near_mate = swap(near, "seq", 1)
    span = columns // CUTS
    pieces = []
    for cut in range(CUTS):
        share = span // 2 if cut == 0 else span
        far = []
        for start in range(cut * span, (cut + 1) * span, share):
            far.append(swap(out_weight[:, start : start + share], "seq", 2 * inner))
        far = far[0] if len(far) == 1 else jnp.concatenate(far, axis=1)
        far_near = swap(far, "seq", 2)
        far_mate = swap(far, "seq", 1)
        far_near_mate = swap(far_near, "seq", 1)
        pieces.append(
            [out_weight, mate, near, near_mate, far, far_mate, far_near, far_near_mate]
        )
    masks = [0, 1, 2, 3, 2 * inner, 2 * inner + 1, 2 * inner + 2, 2 * inner + 3]
    spots = []
    for mask in masks:
        owner = here ^ mask
        spots.append((owner // (2 * inner) != place) * inner + owner % inner)
    spots = jnp.stack(spots).astype(jnp.int32)

    gain = direct_gain.reshape(2, half // wide, devices // 2, each)
    gain = lax.dynamic_index_in_dim(lax.dynamic_index_in_dim(gain, twin, 0, False), rank, 1, False)
    gain = jnp.broadcast_to(gain.reshape(2 * pairs, 1), (2 * pairs, LANES))

    padded = jnp.pad(edges[0], ((0, PACK - (TAPS - 1)), (0, 0)))
    asked = jnp.concatenate([query_feat, padded], axis=0)
    asked = lax.dynamic_slice_in_dim(asked, (1 - twin) * half, half, 1)
    asked = swap(asked, "seq", inner)
    asked_edge = asked[tokens : tokens + TAPS - 1]

    def at(i):
        return (i // (2 * inner) * inner + i % inner) * 2 + i // inner % 2

    groups = [[o * 2 * inner + t * inner + i for o in range(outer) for i in range(inner)] for t in range(2)]
    spreads, backs, kept, given = [], [], [], []
    for start, blocks in zip(starts, parts):
        turned = mix(
            key_feat, value_feat, edges, short_filter, start, blocks, wide, outer, inner, long_filter
        )
        turned = turned.reshape(devices, blocks * (each + each // 2), tokens)
        spreads.append(lax.all_to_all(turned, "seq", split_axis=0, concat_axis=0, tiled=True))
    for part, (start, blocks) in enumerate(zip(starts, parts)):
        width = min(16, each)
        per = each // width
        conv = convolve(
            spreads[part],
            spreads[part],
            blocks * each,
            gain,
            at,
            lambda g: g // per * (3 * per // 2) + g % per,
            lambda g: g // per * (3 * per) + 2 * per + g % per,
            lambda g: start * per + g,
        )
        conv = conv.reshape(devices // 2, 2, blocks * each, tokens)
        backs.append(
            lax.all_to_all(conv, "seq", split_axis=0, concat_axis=0, tiled=True, axis_index_groups=groups)
        )
    blocks = half // wide
    spot = jnp.stack([twin * blocks, twin * blocks, twin, 0 * twin, 1 - twin]).astype(jnp.int32)
    for part, start in enumerate(starts):
        own, passed = gate(spot, short_filter, backs[part], start, wide, (query_feat, edges[0]), (asked, asked_edge))
        kept.append(own)
        given.append(passed)
    kept_far, given_far = [], []
    for part in range(len(parts)):
        given_far.append(swap(given[part], "ch", 1))
        kept_far.append(swap(kept[part], "ch", 1))
    sums, taken = [], []
    for cut in range(CUTS):
        held, passed = project(
            spots, kept + kept_far, given + given_far, pieces[cut], span, cut * span
        )
        sums.append(held)
        taken.append(swap(passed, "seq", inner))
    outs = [(a + b.astype(jnp.float32)).astype(jnp.bfloat16) for a, b in zip(sums, taken)]
    return jnp.concatenate(outs, axis=1)


def solution(mesh):
    in_specs = (
        P("seq", "ch"),
        P("seq", "ch"),
        P("seq", "ch"),
        P(None, None, "ch"),
        P("ch", "seq"),
        P("ch"),
        P("seq", "ch"),
    )
    return jax.shard_map(layer, mesh=mesh, in_specs=in_specs, out_specs=P("seq", "ch"), check_vma=False)
```

```python
import functools

import jax
import jax.numpy as jnp
from jax import lax
from jax.experimental import pallas as pl
from jax.experimental.pallas import tpu as pltpu
from jax.sharding import PartitionSpec as P


TAPS = 3
PARTS = (1, 1)
CUTS = 2
LANES = 128
PACK = 16


def shifted(block, axis, distance):
    devices = range(lax.axis_size(axis))
    route = [(i - distance, i) for i in devices if i - distance in devices]
    return lax.ppermute(block, axis, route)


def featurized(inputs, edge, taps):
    rows = inputs.astype(jnp.float32)
    index = lax.broadcasted_iota(jnp.int32, rows.shape, 0)
    total = taps[0:1] * rows
    for tap in range(1, TAPS):
        moved = pltpu.roll(rows, tap, 0)
        for row in range(tap):
            first = TAPS - 1 - tap + row
            moved = jnp.where(index == row, edge[first : first + 1], moved)
        total = total + taps[tap : tap + 1] * moved
    return total


def mix_kernel(wide, key_ref, value_ref, edge_ref, short_ref, *refs):
    sent_ref = refs[-1]
    outer, _, inner, _, tokens = sent_ref.shape
    edge = edge_ref[...].astype(jnp.float32)
    mixed = featurized(key_ref[...], edge[1], short_ref[1]) * featurized(
        value_ref[...], edge[2], short_ref[2]
    )
    each = wide // (outer * inner)
    turned = mixed.T.astype(jnp.bfloat16)
    row = 0
    for block in range(mixed.shape[1] // wide):
        part = turned[block * wide : (block + 1) * wide]
        sent_ref[:, 0, :, row : row + each, :] = part.reshape(outer, inner, each, tokens)
        row += each
        for taps_ref in refs[:-1]:
            half = wide // 2
            taps = taps_ref[block * half : (block + 1) * half, :].astype(jnp.bfloat16)
            sent_ref[:, 0, :, row : row + each // 2, :] = taps.reshape(outer, inner, each // 2, tokens)
            row += each // 2


def gate_kernel(count, *refs):
    short_ref = refs[0]
    for own in range(count):
        query_ref, edge_ref, conv_ref = refs[1 + 3 * own : 4 + 3 * own]
        gated_ref = refs[1 + 3 * count + own]
        edge = edge_ref[...].astype(jnp.float32)
        query_short = featurized(query_ref[...], edge, short_ref[0])
        wide, tokens = query_short.shape[1], query_short.shape[0]
        summed = conv_ref[...].astype(jnp.float32).reshape(wide, tokens).T
        gated_ref[0] = (query_short * summed).astype(jnp.bfloat16)


def conv_kernel(n, tok, width, place, x_ref, f_ref, gain_ref, y_ref, xi, xs, ys, fs):
    halves = tok // LANES
    groups = LANES // PACK
    for e in range(halves):
        for i in range(n):
            fs[:, i * halves + e, :] = f_ref[i, :, e * LANES : (e + 1) * LANES].astype(jnp.float32)
            xi[e, i * width : (i + 1) * width, :] = x_ref[
                i, :, e * LANES : (e + 1) * LANES
            ].astype(jnp.float32)
        for c in range(width):
            xs[e, c, 0:n, :] = jnp.zeros((n, LANES), jnp.float32)
            xs[e, c, n : 2 * n, :] = xi[e, pl.ds(c, n, stride=width), :]
    lane = lax.broadcasted_iota(jnp.int32, (PACK, LANES), 1)
    sub = lax.broadcasted_iota(jnp.int32, (PACK, LANES), 0)

    def one(p, carry):
        def skewed(m):
            if m == 0:
                return jnp.zeros((PACK, LANES), jnp.float32)
            row = fs[p, m - 1 : m, :]
            return pltpu.roll(
                jnp.broadcast_to(row, (PACK, LANES)), 0, 1, stride=1, stride_axis=0
            )

        def turns(m, part):
            now = skewed(m)
            base = jnp.where(lane >= sub, now, part).astype(jnp.bfloat16)
            return now, [base] + [
                pltpu.roll(base, LANES - PACK * k, 1) for k in range(1, groups)
            ]

        def stack(before, after):
            tiles = [after[0]]
            for k in range(groups - 1, 0, -1):
                tiles.append(jnp.where(lane < LANES - PACK * k, before[k], after[k]))
            return jnp.concatenate(tiles, axis=0)

        part, before = turns(0, skewed(0))
        old = jnp.zeros((LANES, LANES), jnp.bfloat16)
        acc = None
        for d in range(n):
            cols = [old]
            for e in range(halves):
                part, after = turns(d * halves + e + 1, part)
                cols.append(stack(before, after))
                before = after
            old = cols[-1]
            rhs = jnp.concatenate(
                [jnp.concatenate(cols[1:], axis=1), jnp.concatenate(cols[:-1], axis=1)], axis=0
            )
            lhs = jnp.concatenate(
                [
                    jnp.concatenate(
                        [
                            xs[e, 2 * p + c, n - d : 2 * n - d, :].astype(jnp.bfloat16)
                            for e in range(halves)
                        ],
                        axis=1,
                    )
                    for c in range(2)
                ],
                axis=0,
            )
            out = jnp.dot(lhs, rhs, preferred_element_type=jnp.float32)
            acc = out if acc is None else acc + out
        for e in range(halves):
            for c in range(2):
                ys[e, pl.ds(2 * p + c, n, stride=width), :] = acc[
                    c * n : (c + 1) * n, e * LANES : (e + 1) * LANES
                ]
        return carry

    lax.fori_loop(0, width // 2, one, 0, unroll=4 if n <= 16 else 1)
    for e in range(halves):
        for i in range(n):
            rows = slice(i * width, (i + 1) * width)
            total = ys[e, rows, :] + gain_ref[...] * xi[e, rows, :]
            y_ref[place(i), :, e * LANES : (e + 1) * LANES] = total.astype(jnp.bfloat16)


def convolve(x, f, chans, gain, place, x_at, f_at, gain_at):
    n, _, tok = x.shape
    width = min(16, chans)
    halves = tok // LANES
    assert halves == 2
    return pl.pallas_call(
        functools.partial(conv_kernel, n, tok, width, place),
        grid=(chans // width,),
        in_specs=[
            pl.BlockSpec((n, width, tok), lambda g: (0, x_at(g), 0)),
            pl.BlockSpec((n, width // 2, tok), lambda g: (0, f_at(g), 0)),
            pl.BlockSpec((width, LANES), lambda g: (gain_at(g), 0)),
        ],
        out_specs=pl.BlockSpec((n, width, tok), lambda g: (0, g, 0)),
        out_shape=jax.ShapeDtypeStruct((n, chans, tok), jnp.bfloat16),
        scratch_shapes=[
            pltpu.VMEM((halves, n * width, LANES), jnp.float32),
            pltpu.VMEM((halves, width, 2 * n, LANES), jnp.float32),
            pltpu.VMEM((halves, n * width, LANES), jnp.float32),
            pltpu.VMEM((width // 2, n * halves, LANES), jnp.float32),
        ],
        name="convolve",
    )(x, f, gain)


def mix(key_feat, value_feat, edges, short_filter, start, blocks, wide, outer, inner, *taps):
    tokens, channels = key_feat.shape
    each = wide // (outer * inner)
    each += each // 2 * len(taps)
    per = channels // (2 * wide)
    many = 2 if start % 2 == blocks % 2 == per % 2 == 0 else 1
    rows = pl.BlockSpec((tokens, many * wide), lambda t, g: (0, (t * per + start) // many + g))
    return pl.pallas_call(
        functools.partial(mix_kernel, wide),
        grid=(2, blocks // many),
        in_specs=[
            rows,
            rows,
            pl.BlockSpec((3, TAPS - 1, many * wide), lambda t, g: (0, 0, (t * per + start) // many + g)),
            pl.BlockSpec((3, TAPS, many * wide), lambda t, g: (0, 0, (t * per + start) // many + g)),
        ]
        + [pl.BlockSpec((many * wide // 2, tokens), lambda t, g: ((t * per + start) // many + g, 0))]
        * len(taps),
        out_specs=pl.BlockSpec((outer, 1, inner, many * each, tokens), lambda t, g: (0, t, 0, g, 0)),
        out_shape=jax.ShapeDtypeStruct((outer, 2, inner, blocks * each, tokens), jnp.bfloat16),
        name="mix",
    )(key_feat, value_feat, edges, short_filter, *taps)


def gate(spot, short_filter, conv, first, wide, *sources):
    count = len(sources)
    origins, _, chans, tokens = conv.shape
    blocks = origins * chans // wide
    each = max(wide // origins, 1)
    each = each if chans % each == 0 and each % 8 == 0 else chans
    per = wide // each
    specs, operands = [], []
    for own, (query, edge) in enumerate(sources):
        column = lambda g, spot, own=own: (0, spot[1 + 2 * own] + g + first)

        def part(g, spot, own=own):
            return (0, spot[2 + 2 * own], g, 0) if per == origins else (g, spot[2 + 2 * own], 0, 0)

        specs += [
            pl.BlockSpec((tokens, wide), column),
            pl.BlockSpec((TAPS - 1, wide), column),
            pl.BlockSpec((per, 1, each, tokens), part),
        ]
        operands += [query, edge, conv]
    return pl.pallas_call(
        lambda spot_ref, *refs: gate_kernel(count, *refs),
        grid_spec=pltpu.PrefetchScalarGridSpec(
            num_scalar_prefetch=1,
            grid=(blocks,),
            in_specs=[pl.BlockSpec((3, TAPS, wide), lambda g, spot: (0, 0, spot[0] + g + first))] + specs,
            out_specs=[pl.BlockSpec((1, tokens, wide), lambda g, spot: (g, 0, 0))] * count,
        ),
        out_shape=[jax.ShapeDtypeStruct((blocks, tokens, wide), jnp.bfloat16)] * count,
        name="gate",
    )(spot, short_filter, *operands)


def plain(query_feat, key_feat, value_feat, short_filter, long_filter, direct_gain, out_weight):
    tokens, channels = query_feat.shape
    devices = lax.axis_size("seq")
    pairs = long_filter.shape[0] // devices
    here = lax.axis_index("seq")
    weights = lax.all_gather(out_weight, "seq", axis=0, tiled=True)
    last = slice(tokens - (TAPS - 1), None)
    edges = shifted(jnp.stack([query_feat[last], key_feat[last], value_feat[last]]), "seq", 1)
    sent = long_filter.astype(jnp.bfloat16).reshape(devices, pairs, tokens)
    taps = lax.all_to_all(sent, "seq", split_axis=0, concat_axis=0, tiled=True)
    gain = lax.dynamic_index_in_dim(direct_gain.reshape(devices, 2 * pairs, 1), here, 0, False)
    gain = jnp.broadcast_to(gain, (2 * pairs, LANES))
    turned = mix(key_feat, value_feat, edges, short_filter, 0, 1, channels // 2, 1, devices // 2)
    turned = turned.reshape(devices, 2 * pairs, tokens)
    spread = lax.all_to_all(turned, "seq", split_axis=0, concat_axis=0, tiled=True)
    same = lambda i: i
    conv = convolve(spread, taps, 2 * pairs, gain, same, same, same, same)
    conv = lax.all_to_all(conv, "seq", split_axis=0, concat_axis=0, tiled=True)
    wide = min(256, channels)
    spot = jnp.zeros((3,), jnp.int32)
    (gated,) = gate(spot, short_filter, conv[:, None], 0, wide, (query_feat, edges[0]))
    gated = gated.transpose(1, 0, 2).reshape(tokens, channels)
    features = lax.all_gather(gated, "ch", axis=1, tiled=True)
    return jnp.dot(features, weights, preferred_element_type=jnp.float32).astype(jnp.bfloat16)


def project_kernel(count, per, spots, *refs):
    gated, pieces = refs[:per], refs[per : per + count]
    out_ref, rows = refs[per + count :]
    wide = gated[0].shape[2]
    places = [(source, block) for source in range(per) for block in range(gated[source].shape[0])]

    @pl.when(pl.program_id(0) == 0)
    def _():
        for piece in range(count):
            spot = spots[piece]
            for value, (source, block) in enumerate(places):

                @pl.when(spot == value)
                def _():
                    rows[:, piece * wide : (piece + 1) * wide] = gated[source][block]

    total = None
    for piece in range(count):
        out = jnp.dot(
            rows[:, piece * wide : (piece + 1) * wide],
            pieces[piece][...],
            preferred_element_type=jnp.float32,
        )
        total = out if total is None else total + out
    out_ref[...] = total.astype(out_ref.dtype)


def project(spots, gated, pieces, columns, first, kind):
    tokens, wide = gated[0].shape[1:]
    count = len(pieces)
    step = min(512, columns)

    def held(piece):
        skip = first // step if piece.shape[1] > columns else 0
        return pl.BlockSpec((wide, step), lambda j, spots: (0, j + skip))

    return pl.pallas_call(
        functools.partial(project_kernel, count, len(gated)),
        grid_spec=pltpu.PrefetchScalarGridSpec(
            num_scalar_prefetch=1,
            grid=(columns // step,),
            in_specs=[pl.BlockSpec(block.shape, lambda j, spots: (0, 0, 0)) for block in gated]
            + [held(piece) for piece in pieces],
            out_specs=pl.BlockSpec((tokens, step), lambda j, spots: (0, j)),
            scratch_shapes=[pltpu.VMEM((tokens, count * wide), jnp.bfloat16)],
        ),
        out_shape=jax.ShapeDtypeStruct((tokens, columns), kind),
        name="project",
    )(spots, *gated, *pieces)


def layer(query_feat, key_feat, value_feat, short_filter, long_filter, direct_gain, out_weight):
    tokens, channels = query_feat.shape
    devices = lax.axis_size("seq")
    sides = lax.axis_size("ch")
    here = lax.axis_index("seq")
    place = lax.axis_index("ch")
    depth, columns = out_weight.shape
    pairs = long_filter.shape[0] // devices
    inner, outer = 4, devices // 8
    small = sides == 2 and outer == 2 and depth % 256 == 0
    if not small:
        return plain(query_feat, key_feat, value_feat, short_filter, long_filter, direct_gain, out_weight)
    half = channels // 2
    wide = depth
    parts = [half // wide * share // sum(PARTS) for share in PARTS]
    starts = [sum(parts[:part]) for part in range(len(parts))]
    each = wide // (devices // 2)
    twin = here // inner % 2
    rank = here // (2 * inner) * inner + here % inner

    def swap(block, axis, mask):
        return lax.ppermute(block, axis, [(i ^ mask, i) for i in range(lax.axis_size(axis))])

    last = slice(tokens - (TAPS - 1), None)
    edges = shifted(jnp.stack([query_feat[last], key_feat[last], value_feat[last]]), "seq", 1)

    near = swap(out_weight, "seq", 2)
    mate = swap(out_weight, "seq", 1)
    near_mate = swap(near, "seq", 1)
    span = columns // CUTS
    pieces = []
    for cut in range(CUTS):
        share = span // 2 if cut == 0 else span
        far = []
        for start in range(cut * span, (cut + 1) * span, share):
            far.append(swap(out_weight[:, start : start + share], "seq", 2 * inner))
        far = far[0] if len(far) == 1 else jnp.concatenate(far, axis=1)
        far_near = swap(far, "seq", 2)
        far_mate = swap(far, "seq", 1)
        far_near_mate = swap(far_near, "seq", 1)
        pieces.append(
            [out_weight, mate, near, near_mate, far, far_mate, far_near, far_near_mate]
        )
    masks = [0, 1, 2, 3, 2 * inner, 2 * inner + 1, 2 * inner + 2, 2 * inner + 3]
    spots = []
    for mask in masks:
        owner = here ^ mask
        spots.append((owner // (2 * inner) != place) * inner + owner % inner)
    spots = jnp.stack(spots).astype(jnp.int32)

    gain = direct_gain.reshape(2, half // wide, devices // 2, each)
    gain = lax.dynamic_index_in_dim(lax.dynamic_index_in_dim(gain, twin, 0, False), rank, 1, False)
    gain = jnp.broadcast_to(gain.reshape(2 * pairs, 1), (2 * pairs, LANES))

    padded = jnp.pad(edges[0], ((0, PACK - (TAPS - 1)), (0, 0)))
    asked = jnp.concatenate([query_feat, padded], axis=0)
    asked = lax.dynamic_slice_in_dim(asked, (1 - twin) * half, half, 1)
    asked = swap(asked, "seq", inner)
    asked_edge = asked[tokens : tokens + TAPS - 1]

    def at(i):
        return (i // (2 * inner) * inner + i % inner) * 2 + i // inner % 2

    groups = [[o * 2 * inner + t * inner + i for o in range(outer) for i in range(inner)] for t in range(2)]
    spreads, backs, kept, given = [], [], [], []
    for start, blocks in zip(starts, parts):
        turned = mix(
            key_feat, value_feat, edges, short_filter, start, blocks, wide, outer, inner, long_filter
        )
        turned = turned.reshape(devices, blocks * (each + each // 2), tokens)
        spreads.append(lax.all_to_all(turned, "seq", split_axis=0, concat_axis=0, tiled=True))
    for part, (start, blocks) in enumerate(zip(starts, parts)):
        width = min(16, each)
        per = each // width
        conv = convolve(
            spreads[part],
            spreads[part],
            blocks * each,
            gain,
            at,
            lambda g: g // per * (3 * per // 2) + g % per,
            lambda g: g // per * (3 * per) + 2 * per + g % per,
            lambda g: start * per + g,
        )
        conv = conv.reshape(devices // 2, 2, blocks * each, tokens)
        backs.append(
            lax.all_to_all(conv, "seq", split_axis=0, concat_axis=0, tiled=True, axis_index_groups=groups)
        )
    blocks = half // wide
    spot = jnp.stack([twin * blocks, twin * blocks, twin, 0 * twin, 1 - twin]).astype(jnp.int32)
    for part, start in enumerate(starts):
        own, passed = gate(spot, short_filter, backs[part], start, wide, (query_feat, edges[0]), (asked, asked_edge))
        kept.append(own)
        given.append(passed)
    kept_far, given_far = [], []
    for part in range(len(parts)):
        given_far.append(swap(given[part], "ch", 1))
        kept_far.append(swap(kept[part], "ch", 1))
    sums, taken = [], []
    for cut in range(CUTS):
        passed = project(spots, given + given_far, pieces[cut], span, cut * span, jnp.bfloat16)
        taken.append(swap(passed, "seq", inner))
    for cut in range(CUTS):
        sums.append(project(spots, kept + kept_far, pieces[cut], span, cut * span, jnp.float32))
    outs = [(a + b.astype(jnp.float32)).astype(jnp.bfloat16) for a, b in zip(sums, taken)]
    return jnp.concatenate(outs, axis=1)


def solution(mesh):
    in_specs = (
        P("seq", "ch"),
        P("seq", "ch"),
        P("seq", "ch"),
        P(None, None, "ch"),
        P("ch", "seq"),
        P("ch"),
        P("seq", "ch"),
    )
    return jax.shard_map(layer, mesh=mesh, in_specs=in_specs, out_specs=P("seq", "ch"), check_vma=False)
```

```python
import functools

import jax
import jax.numpy as jnp
from jax import lax
from jax.experimental import pallas as pl
from jax.experimental.pallas import tpu as pltpu
from jax.sharding import PartitionSpec as P


TAPS = 3
PARTS = (1, 1)
CUTS = 2
LANES = 128
PACK = 16


def shifted(block, axis, distance):
    devices = range(lax.axis_size(axis))
    route = [(i - distance, i) for i in devices if i - distance in devices]
    return lax.ppermute(block, axis, route)


def featurized(inputs, edge, taps):
    rows = inputs.astype(jnp.float32)
    index = lax.broadcasted_iota(jnp.int32, rows.shape, 0)
    total = taps[0:1] * rows
    for tap in range(1, TAPS):
        moved = pltpu.roll(rows, tap, 0)
        for row in range(tap):
            first = TAPS - 1 - tap + row
            moved = jnp.where(index == row, edge[first : first + 1], moved)
        total = total + taps[tap : tap + 1] * moved
    return total


def mix_kernel(wide, key_ref, value_ref, edge_ref, short_ref, *refs):
    sent_ref = refs[-1]
    outer, _, inner, _, tokens = sent_ref.shape
    edge = edge_ref[...].astype(jnp.float32)
    mixed = featurized(key_ref[...], edge[1], short_ref[1]) * featurized(
        value_ref[...], edge[2], short_ref[2]
    )
    each = wide // (outer * inner)
    turned = mixed.T.astype(jnp.bfloat16)
    row = 0
    for block in range(mixed.shape[1] // wide):
        part = turned[block * wide : (block + 1) * wide]
        sent_ref[:, 0, :, row : row + each, :] = part.reshape(outer, inner, each, tokens)
        row += each
        for taps_ref in refs[:-1]:
            half = wide // 2
            taps = taps_ref[block * half : (block + 1) * half, :].astype(jnp.bfloat16)
            sent_ref[:, 0, :, row : row + each // 2, :] = taps.reshape(outer, inner, each // 2, tokens)
            row += each // 2


def gate_kernel(count, *refs):
    short_ref = refs[0]
    for own in range(count):
        query_ref, edge_ref, conv_ref = refs[1 + 3 * own : 4 + 3 * own]
        gated_ref = refs[1 + 3 * count + own]
        edge = edge_ref[...].astype(jnp.float32)
        query_short = featurized(query_ref[...], edge, short_ref[0])
        wide, tokens = query_short.shape[1], query_short.shape[0]
        summed = conv_ref[...].astype(jnp.float32).reshape(wide, tokens).T
        gated_ref[0] = (query_short * summed).astype(jnp.bfloat16)


def conv_kernel(n, tok, width, place, x_ref, f_ref, gain_ref, y_ref, xi, xs, ys, fs):
    halves = tok // LANES
    groups = LANES // PACK
    for e in range(halves):
        for i in range(n):
            fs[:, i * halves + e, :] = f_ref[i, :, e * LANES : (e + 1) * LANES].astype(jnp.float32)
            xi[e, i * width : (i + 1) * width, :] = x_ref[
                i, :, e * LANES : (e + 1) * LANES
            ].astype(jnp.float32)
        for c in range(width):
            xs[e, c, 0:n, :] = jnp.zeros((n, LANES), jnp.float32)
            xs[e, c, n : 2 * n, :] = xi[e, pl.ds(c, n, stride=width), :]
    lane = lax.broadcasted_iota(jnp.int32, (PACK, LANES), 1)
    sub = lax.broadcasted_iota(jnp.int32, (PACK, LANES), 0)

    def one(p, carry):
        def skewed(m):
            if m == 0:
                return jnp.zeros((PACK, LANES), jnp.float32)
            row = fs[p, m - 1 : m, :]
            return pltpu.roll(
                jnp.broadcast_to(row, (PACK, LANES)), 0, 1, stride=1, stride_axis=0
            )

        def turns(m, part):
            now = skewed(m)
            base = jnp.where(lane >= sub, now, part).astype(jnp.bfloat16)
            return now, [base] + [
                pltpu.roll(base, LANES - PACK * k, 1) for k in range(1, groups)
            ]

        def stack(before, after):
            tiles = [after[0]]
            for k in range(groups - 1, 0, -1):
                tiles.append(jnp.where(lane < LANES - PACK * k, before[k], after[k]))
            return jnp.concatenate(tiles, axis=0)

        part, before = turns(0, skewed(0))
        old = jnp.zeros((LANES, LANES), jnp.bfloat16)
        acc = None
        for d in range(n):
            cols = [old]
            for e in range(halves):
                part, after = turns(d * halves + e + 1, part)
                cols.append(stack(before, after))
                before = after
            old = cols[-1]
            rhs = jnp.concatenate(
                [jnp.concatenate(cols[1:], axis=1), jnp.concatenate(cols[:-1], axis=1)], axis=0
            )
            lhs = jnp.concatenate(
                [
                    jnp.concatenate(
                        [
                            xs[e, 2 * p + c, n - d : 2 * n - d, :].astype(jnp.bfloat16)
                            for e in range(halves)
                        ],
                        axis=1,
                    )
                    for c in range(2)
                ],
                axis=0,
            )
            out = jnp.dot(lhs, rhs, preferred_element_type=jnp.float32)
            acc = out if acc is None else acc + out
        for e in range(halves):
            for c in range(2):
                ys[e, pl.ds(2 * p + c, n, stride=width), :] = acc[
                    c * n : (c + 1) * n, e * LANES : (e + 1) * LANES
                ]
        return carry

    lax.fori_loop(0, width // 2, one, 0, unroll=4 if n <= 16 else 1)
    for e in range(halves):
        for i in range(n):
            rows = slice(i * width, (i + 1) * width)
            total = ys[e, rows, :] + gain_ref[...] * xi[e, rows, :]
            y_ref[place(i), :, e * LANES : (e + 1) * LANES] = total.astype(jnp.bfloat16)


def convolve(x, f, chans, gain, place, x_at, f_at, gain_at):
    n, _, tok = x.shape
    width = min(16, chans)
    halves = tok // LANES
    assert halves == 2
    return pl.pallas_call(
        functools.partial(conv_kernel, n, tok, width, place),
        grid=(chans // width,),
        in_specs=[
            pl.BlockSpec((n, width, tok), lambda g: (0, x_at(g), 0)),
            pl.BlockSpec((n, width // 2, tok), lambda g: (0, f_at(g), 0)),
            pl.BlockSpec((width, LANES), lambda g: (gain_at(g), 0)),
        ],
        out_specs=pl.BlockSpec((n, width, tok), lambda g: (0, g, 0)),
        out_shape=jax.ShapeDtypeStruct((n, chans, tok), jnp.bfloat16),
        scratch_shapes=[
            pltpu.VMEM((halves, n * width, LANES), jnp.float32),
            pltpu.VMEM((halves, width, 2 * n, LANES), jnp.float32),
            pltpu.VMEM((halves, n * width, LANES), jnp.float32),
            pltpu.VMEM((width // 2, n * halves, LANES), jnp.float32),
        ],
        name="convolve",
    )(x, f, gain)


def mix(key_feat, value_feat, edges, short_filter, start, blocks, wide, outer, inner, *taps):
    tokens, channels = key_feat.shape
    each = wide // (outer * inner)
    each += each // 2 * len(taps)
    per = channels // (2 * wide)
    many = 2 if start % 2 == blocks % 2 == per % 2 == 0 else 1
    rows = pl.BlockSpec((tokens, many * wide), lambda t, g: (0, (t * per + start) // many + g))
    return pl.pallas_call(
        functools.partial(mix_kernel, wide),
        grid=(2, blocks // many),
        in_specs=[
            rows,
            rows,
            pl.BlockSpec((3, TAPS - 1, many * wide), lambda t, g: (0, 0, (t * per + start) // many + g)),
            pl.BlockSpec((3, TAPS, many * wide), lambda t, g: (0, 0, (t * per + start) // many + g)),
        ]
        + [pl.BlockSpec((many * wide // 2, tokens), lambda t, g: ((t * per + start) // many + g, 0))]
        * len(taps),
        out_specs=pl.BlockSpec((outer, 1, inner, many * each, tokens), lambda t, g: (0, t, 0, g, 0)),
        out_shape=jax.ShapeDtypeStruct((outer, 2, inner, blocks * each, tokens), jnp.bfloat16),
        name="mix",
    )(key_feat, value_feat, edges, short_filter, *taps)


def gate(spot, short_filter, conv, first, wide, *sources):
    count = len(sources)
    origins, _, chans, tokens = conv.shape
    blocks = origins * chans // wide
    each = max(wide // origins, 1)
    each = each if chans % each == 0 and each % 8 == 0 else chans
    per = wide // each
    specs, operands = [], []
    for own, (query, edge) in enumerate(sources):
        column = lambda g, spot, own=own: (0, spot[1 + 2 * own] + g + first)

        def part(g, spot, own=own):
            return (0, spot[2 + 2 * own], g, 0) if per == origins else (g, spot[2 + 2 * own], 0, 0)

        specs += [
            pl.BlockSpec((tokens, wide), column),
            pl.BlockSpec((TAPS - 1, wide), column),
            pl.BlockSpec((per, 1, each, tokens), part),
        ]
        operands += [query, edge, conv]
    return pl.pallas_call(
        lambda spot_ref, *refs: gate_kernel(count, *refs),
        grid_spec=pltpu.PrefetchScalarGridSpec(
            num_scalar_prefetch=1,
            grid=(blocks,),
            in_specs=[pl.BlockSpec((3, TAPS, wide), lambda g, spot: (0, 0, spot[0] + g + first))] + specs,
            out_specs=[pl.BlockSpec((1, tokens, wide), lambda g, spot: (g, 0, 0))] * count,
        ),
        out_shape=[jax.ShapeDtypeStruct((blocks, tokens, wide), jnp.bfloat16)] * count,
        name="gate",
    )(spot, short_filter, *operands)


def plain(query_feat, key_feat, value_feat, short_filter, long_filter, direct_gain, out_weight):
    tokens, channels = query_feat.shape
    devices = lax.axis_size("seq")
    pairs = long_filter.shape[0] // devices
    here = lax.axis_index("seq")
    weights = lax.all_gather(out_weight, "seq", axis=0, tiled=True)
    last = slice(tokens - (TAPS - 1), None)
    edges = shifted(jnp.stack([query_feat[last], key_feat[last], value_feat[last]]), "seq", 1)
    sent = long_filter.astype(jnp.bfloat16).reshape(devices, pairs, tokens)
    taps = lax.all_to_all(sent, "seq", split_axis=0, concat_axis=0, tiled=True)
    gain = lax.dynamic_index_in_dim(direct_gain.reshape(devices, 2 * pairs, 1), here, 0, False)
    gain = jnp.broadcast_to(gain, (2 * pairs, LANES))
    turned = mix(key_feat, value_feat, edges, short_filter, 0, 1, channels // 2, 1, devices // 2)
    turned = turned.reshape(devices, 2 * pairs, tokens)
    spread = lax.all_to_all(turned, "seq", split_axis=0, concat_axis=0, tiled=True)
    same = lambda i: i
    conv = convolve(spread, taps, 2 * pairs, gain, same, same, same, same)
    conv = lax.all_to_all(conv, "seq", split_axis=0, concat_axis=0, tiled=True)
    wide = min(256, channels)
    spot = jnp.zeros((3,), jnp.int32)
    (gated,) = gate(spot, short_filter, conv[:, None], 0, wide, (query_feat, edges[0]))
    gated = gated.transpose(1, 0, 2).reshape(tokens, channels)
    features = lax.all_gather(gated, "ch", axis=1, tiled=True)
    return jnp.dot(features, weights, preferred_element_type=jnp.float32).astype(jnp.bfloat16)


def project_kernel(count, per, spots, *refs):
    gated, pieces = refs[:per], refs[per : per + count]
    out_ref, rows = refs[per + count :]
    wide = gated[0].shape[2]
    places = [(source, block) for source in range(per) for block in range(gated[source].shape[0])]

    @pl.when(pl.program_id(0) == 0)
    def _():
        for piece in range(count):
            spot = spots[piece]
            for value, (source, block) in enumerate(places):

                @pl.when(spot == value)
                def _():
                    rows[:, piece * wide : (piece + 1) * wide] = gated[source][block]

    total = None
    for piece in range(count):
        out = jnp.dot(
            rows[:, piece * wide : (piece + 1) * wide],
            pieces[piece][...],
            preferred_element_type=jnp.float32,
        )
        total = out if total is None else total + out
    out_ref[...] = total.astype(out_ref.dtype)


def project(spots, gated, pieces, columns, first, kind):
    tokens, wide = gated[0].shape[1:]
    count = len(pieces)
    step = min(512, columns)

    def held(piece):
        skip = first // step if piece.shape[1] > columns else 0
        return pl.BlockSpec((wide, step), lambda j, spots: (0, j + skip))

    return pl.pallas_call(
        functools.partial(project_kernel, count, len(gated)),
        grid_spec=pltpu.PrefetchScalarGridSpec(
            num_scalar_prefetch=1,
            grid=(columns // step,),
            in_specs=[pl.BlockSpec(block.shape, lambda j, spots: (0, 0, 0)) for block in gated]
            + [held(piece) for piece in pieces],
            out_specs=pl.BlockSpec((tokens, step), lambda j, spots: (0, j)),
            scratch_shapes=[pltpu.VMEM((tokens, count * wide), jnp.bfloat16)],
        ),
        out_shape=jax.ShapeDtypeStruct((tokens, columns), kind),
        name="project",
    )(spots, *gated, *pieces)


def layer(query_feat, key_feat, value_feat, short_filter, long_filter, direct_gain, out_weight):
    tokens, channels = query_feat.shape
    devices = lax.axis_size("seq")
    sides = lax.axis_size("ch")
    here = lax.axis_index("seq")
    place = lax.axis_index("ch")
    depth, columns = out_weight.shape
    pairs = long_filter.shape[0] // devices
    inner, outer = 4, devices // 8
    small = sides == 2 and outer == 2 and depth % 256 == 0
    if not small:
        return plain(query_feat, key_feat, value_feat, short_filter, long_filter, direct_gain, out_weight)
    half = channels // 2
    wide = depth
    parts = [half // wide * share // sum(PARTS) for share in PARTS]
    starts = [sum(parts[:part]) for part in range(len(parts))]
    each = wide // (devices // 2)
    twin = here // inner % 2
    rank = here // (2 * inner) * inner + here % inner

    def swap(block, axis, mask):
        return lax.ppermute(block, axis, [(i ^ mask, i) for i in range(lax.axis_size(axis))])

    last = slice(tokens - (TAPS - 1), None)
    edges = shifted(jnp.stack([query_feat[last], key_feat[last], value_feat[last]]), "seq", 1)

    near = swap(out_weight, "seq", 2)
    mate = swap(out_weight, "seq", 1)
    near_mate = swap(near, "seq", 1)
    span = columns // CUTS
    pieces = []
    for cut in range(CUTS):
        share = span // 2 if cut == 0 else span
        far = []
        for start in range(cut * span, (cut + 1) * span, share):
            far.append(swap(out_weight[:, start : start + share], "seq", 2 * inner))
        far = far[0] if len(far) == 1 else jnp.concatenate(far, axis=1)
        far_near = swap(far, "seq", 2)
        far_mate = swap(far, "seq", 1)
        far_near_mate = swap(far_near, "seq", 1)
        pieces.append(
            [out_weight, mate, near, near_mate, far, far_mate, far_near, far_near_mate]
        )
    masks = [0, 1, 2, 3, 2 * inner, 2 * inner + 1, 2 * inner + 2, 2 * inner + 3]
    spots = []
    for mask in masks:
        owner = here ^ mask
        spots.append((owner // (2 * inner) != place) * inner + owner % inner)
    spots = jnp.stack(spots).astype(jnp.int32)

    gain = direct_gain.reshape(2, half // wide, devices // 2, each)
    gain = lax.dynamic_index_in_dim(lax.dynamic_index_in_dim(gain, twin, 0, False), rank, 1, False)
    gain = jnp.broadcast_to(gain.reshape(2 * pairs, 1), (2 * pairs, LANES))

    padded = jnp.pad(edges[0], ((0, PACK - (TAPS - 1)), (0, 0)))
    asked = jnp.concatenate([query_feat, padded], axis=0)
    asked = lax.dynamic_slice_in_dim(asked, (1 - twin) * half, half, 1)
    asked = swap(asked, "seq", inner)
    asked_edge = asked[tokens : tokens + TAPS - 1]

    def at(i):
        return (i // (2 * inner) * inner + i % inner) * 2 + i // inner % 2

    groups = [[o * 2 * inner + t * inner + i for o in range(outer) for i in range(inner)] for t in range(2)]
    spreads, backs, kept, given = [], [], [], []
    for start, blocks in zip(starts, parts):
        turned = mix(
            key_feat, value_feat, edges, short_filter, start, blocks, wide, outer, inner, long_filter
        )
        turned = turned.reshape(devices, blocks * (each + each // 2), tokens)
        spreads.append(lax.all_to_all(turned, "seq", split_axis=0, concat_axis=0, tiled=True))
    for part, (start, blocks) in enumerate(zip(starts, parts)):
        width = min(16, each)
        per = each // width
        conv = convolve(
            spreads[part],
            spreads[part],
            blocks * each,
            gain,
            at,
            lambda g: g // per * (3 * per // 2) + g % per,
            lambda g: g // per * (3 * per) + 2 * per + g % per,
            lambda g: start * per + g,
        )
        conv = conv.reshape(devices // 2, 2, blocks * each, tokens)
        backs.append(
            lax.all_to_all(conv, "seq", split_axis=0, concat_axis=0, tiled=True, axis_index_groups=groups)
        )
    blocks = half // wide
    spot = jnp.stack([twin * blocks, twin * blocks, twin, 0 * twin, 1 - twin]).astype(jnp.int32)
    for part, start in enumerate(starts):
        own, passed = gate(spot, short_filter, backs[part], start, wide, (query_feat, edges[0]), (asked, asked_edge))
        kept.append(own)
        given.append(passed)
    kept_far, given_far = [], []
    for part in range(len(parts)):
        given_far.append(swap(given[part], "ch", 1))
        kept_far.append(swap(kept[part], "ch", 1))
    sums, taken = [], []
    for cut in range(CUTS):
        passed = project(spots, given + given_far, pieces[cut], span, cut * span, jnp.bfloat16)
        taken.append(swap(passed, "seq", inner))
    for cut in range(CUTS):
        sums.append(project(spots, kept + kept_far, pieces[cut], span, cut * span, jnp.float32))
    result = jnp.zeros((tokens, columns), jnp.bfloat16)
    for cut, (ours, theirs) in enumerate(zip(sums, taken)):
        block = (ours + theirs.astype(jnp.float32)).astype(jnp.bfloat16)
        result = lax.dynamic_update_slice(result, block, (0, cut * span))
    return result


def solution(mesh):
    in_specs = (
        P("seq", "ch"),
        P("seq", "ch"),
        P("seq", "ch"),
        P(None, None, "ch"),
        P("ch", "seq"),
        P("ch"),
        P("seq", "ch"),
    )
    return jax.shard_map(layer, mesh=mesh, in_specs=in_specs, out_specs=P("seq", "ch"), check_vma=False)
```
